32 devices in a mesh: section: 16 (over z, y, x), dp: 2 (over core).
Axes of the slice: x: 2, y: 2, z: 4, core: 2. Of those that a mesh axis runs over, the one named last changes fastest.
Arguments:
- pipe_maps: bfloat16 [16, 2, 8, 32, 384], P('section', 'dp'), may hold values from -6 to 6
- fresh_maps: bfloat16 [3, 2, 8, 32, 384], P(None, 'dp'), may hold values from -6 to 6
- teacher_weight: bfloat16 [32, 3, 3, 384, 384], P('section'), may hold values from -0.109375 to 0.109375
- student_depth: float32 [32, 49, 384], P('section'), may hold values from -0.875 to 0.875
- student_point: bfloat16 [32, 384, 384], P('section'), may hold values from -0.3125 to 0.3125
Outputs:
- final_maps: bfloat16 [16, 2, 8, 32, 384], P('section', 'dp')
- point_grad: float32 [32, 384, 384], P('section', None, 'dp')
- depth_grad: float32 [32, 49, 384], P('section', None, 'dp')
The draws below stay inside these ranges and needn't reach their ends.
All inputs are finite; a program needn't handle non-finite values.
Results may differ from the reference program's by a relative error of at most 0.012.
Values may be sent and summed in bfloat16 or wider, within the bound.
A program may use at most 128 MiB of HBM per device.

```python
import jax
import jax.numpy as jnp
from jax import lax

CHANNELS = 384
MAP_H = 8
MAP_W = 32
TAPS = 49
TICKS = 4
BATCH = 2
SECTIONS = 16


def block_scale(rng, extent, shards, smallest, largest):
    gain, own = 1.0, jax.random.fold_in(rng, 6)
    for position, blocks in shards:
        steps = jnp.exp(jax.random.uniform(jax.random.fold_in(own, position), (blocks,), jnp.float32, smallest / len(shards), largest / len(shards)))
        gain = gain * jnp.repeat(steps, extent[position] // blocks).reshape([-1 if axis == position else 1 for axis in range(len(extent))])
    return gain


def noise(stream_key, shape, deviation, limit, split=(), kind=jnp.bfloat16):
    result = deviation * jax.random.normal(stream_key, shape, jnp.float32)
    if split:
        result = result * block_scale(stream_key, shape, split, -0.22, 0.18)
    return jnp.clip(result, -limit, limit).astype(kind)


def setup_inputs(seed: int = 0) -> dict:
    streams_of = jax.random.split(jax.random.key(seed), 6)
    return {
        "pipe_maps": noise(streams_of[0], (SECTIONS, BATCH, MAP_H, MAP_W, CHANNELS), 1.0, 6.0, ((0, 16), (1, 2))),
        "fresh_maps": noise(streams_of[1], (TICKS - 1, BATCH, MAP_H, MAP_W, CHANNELS), 1.0, 6.0, ((1, 2),)),
        "teacher_weight": noise(streams_of[2], (2 * SECTIONS, 3, 3, CHANNELS, CHANNELS), (9 * CHANNELS) ** -0.5, 0.109375, ((0, 16),)),
        "student_depth": noise(streams_of[3], (2 * SECTIONS, TAPS, CHANNELS), TAPS ** -0.5, 0.875, ((0, 16),), jnp.float32),
        "student_point": noise(streams_of[4], (2 * SECTIONS, CHANNELS, CHANNELS), CHANNELS ** -0.5, 0.3125, ((0, 16),)),
    }


def teacher_conv(inmap, kernel):
    batch, height, width, chans = inmap.shape
    padded = jnp.pad(inmap, ((0, 0), (1, 1), (1, 1), (0, 0)))
    total = jnp.zeros((batch * height * width, kernel.shape[-1]), jnp.float32)
    for row in range(3):
        for col in range(3):
            window = padded[:, row:row + height, col:col + width, :].reshape(-1, chans)
            total = total + jnp.dot(window, kernel[row, col], preferred_element_type=jnp.float32)
    return total.reshape(batch, height, width, kernel.shape[-1])

def teacher_pass(inmap, kernels):
    hidden = jnp.maximum(teacher_conv(inmap, kernels[0]), 0.0).astype(jnp.bfloat16)
    summed = inmap.astype(jnp.float32) + teacher_conv(hidden, kernels[1])
    return (0.8 * summed).astype(jnp.bfloat16)

def depth_conv(inmap, taps):
    height, width = (inmap.shape[1], inmap.shape[2])
    padded = jnp.pad(inmap, ((0, 0), (3, 3), (3, 3), (0, 0)))
    total = jnp.zeros(inmap.shape, jnp.float32)
    for row in range(7):
        for col in range(7):
            total = total + padded[:, row:row + height, col:col + width, :] * taps[row * 7 + col]
    return total

def point_apply(gelled, weight):
    chans = weight.shape[0]
    flat = jnp.dot(gelled.reshape(-1, chans), weight, preferred_element_type=jnp.float32)
    return flat.reshape(gelled.shape)

def weight_grad(gelled, upstream):
    chans = gelled.shape[-1]
    return lax.dot_general(gelled.reshape(-1, chans), upstream.reshape(-1, chans), (((0,), (0,)), ((), ())), preferred_element_type=jnp.float32)

def block_back(start_map, act_map, upstream, taps, weight):
    up_bf = upstream.astype(jnp.bfloat16)
    gelled = jax.nn.gelu(act_map).astype(jnp.bfloat16)
    point_part = weight_grad(gelled, up_bf)
    dgel = point_apply(up_bf, weight.T)
    dact = jax.vjp(jax.nn.gelu, act_map)[1](dgel)[0]
    back_map, back_taps = jax.vjp(depth_conv, start_map, taps)[1](dact)
    return (point_part, back_taps, upstream + back_map)

def student_grads(inmap, teach, depth, point):
    area = inmap.shape[1] * inmap.shape[2]
    start_zero = inmap.astype(jnp.float32)
    act_zero = depth_conv(start_zero, depth[0])
    start_one = start_zero + point_apply(jax.nn.gelu(act_zero).astype(jnp.bfloat16), point[0])
    act_one = depth_conv(start_one, depth[1])
    final_map = start_one + point_apply(jax.nn.gelu(act_one).astype(jnp.bfloat16), point[1])
    resid = (final_map - teach.astype(jnp.float32)) * (4.0 / area)
    point_one, taps_one, back_one = block_back(start_one, act_one, resid, depth[1], point[1])
    point_zero, taps_zero, back_zero = block_back(start_zero, act_zero, back_one, depth[0], point[0])
    return (jnp.stack([point_zero, point_one]), jnp.stack([taps_zero, taps_one]))

def reference(pipe_maps, fresh_maps, teacher_weight, student_depth, student_point):
    chans = teacher_weight.shape[-1]
    section_count = pipe_maps.shape[0]
    kernels = teacher_weight.reshape(section_count, 2, 3, 3, chans, chans)
    depth = student_depth.reshape(section_count, 2, student_depth.shape[1], chans)
    point = student_point.reshape(section_count, 2, chans, chans)
    current = pipe_maps
    point_total = jnp.zeros((section_count, 2, chans, chans), jnp.float32)
    depth_total = jnp.zeros((section_count, 2, student_depth.shape[1], chans), jnp.float32)

    def per_section(packed):
        inmap, kern, taps, weight = packed
        teach = teacher_pass(inmap, kern)
        point_part, depth_part = student_grads(inmap, teach, taps, weight)
        return (teach, point_part, depth_part)
    teach_all = current
    for tick_index in range(TICKS):
        teach_all, point_part, depth_part = lax.map(per_section, (current, kernels, depth, point))
        point_total = point_total + point_part
        depth_total = depth_total + depth_part
        if tick_index + 1 < TICKS:
            current = jnp.concatenate([fresh_maps[tick_index][None], teach_all[:-1]], axis=0)
    return (teach_all, point_total.reshape(2 * section_count, chans, chans), depth_total.reshape(2 * section_count, student_depth.shape[1], chans))
```

```python
import functools

import jax
import jax.numpy as jnp
from jax import lax
from jax.experimental import pallas as pl
from jax.experimental.pallas import tpu as pltpu
from jax.sharding import PartitionSpec as P

LANES = 128
F32 = jnp.float32
BF16 = jnp.bfloat16
MESH = pl.DeviceIdType.MESH
NT = (((1,), (1,)), ((), ()))


def lanes(block):
    return slice(block * LANES, (block + 1) * LANES)


def columns(block):
    return pl.ds(pl.multiple_of(block * LANES, LANES), LANES)


def put_padded(vals, pad_ref, height):
    units = vals.shape[0] // (2 * height)
    for block in range(vals.shape[1] // LANES):
        for unit in range(units):
            for half in range(2):
                at = (2 * unit + half) * height
                to = (2 * (unit + half * units) + 1) * height
                pad_ref[block, to : to + height] = vals[at : at + height, lanes(block)]


def spread(pad_ref, out_ref, height, units, reach):
    blocks, taps = out_ref.shape[0], 2 * reach + 1

    def one_row(row, carry):
        for block in range(blocks):

            def load(w):
                return pad_ref[block, pl.ds((2 * w + 1) * height + row - reach, height)]

            zero = jnp.zeros((height, LANES), F32)
            cols = [load(w) for w in range(2 * units)]
            low = [zero] * reach + cols[: units + reach]
            high = cols[units - reach :] + [zero] * reach
            for unit in range(units + 2 * reach):
                out_ref[block, row, unit] = jnp.concatenate([low[unit], high[unit]], axis=0).astype(BF16)
        return carry

    lax.fori_loop(0, taps, one_row, 0)


def tap_sum(src_ref, block, coef_ref, which, start, count, flip):
    total = None
    for rows in ((0, 1, 2, 3), (4, 5, 6)):
        part = None
        for row in rows:
            strip = src_ref[block, row, pl.ds(start, count + 6)]
            acc = None
            for col in range(7):
                tap = row * 7 + col
                tap = 48 - tap if flip else tap
                term = strip[col : col + count] * coef_ref[which, block, tap][None]
                acc = term if acc is None else acc + term
            part = acc if part is None else part + acc
        wide = part.astype(F32)
        total = wide if total is None else total + wide
    return total


def gelu_pair(act):
    root = 0.7978845608028654
    cubic = root * 0.044715
    square = act * act
    tanh = jnp.tanh(act * (root + cubic * square))
    half = 0.5 + 0.5 * tanh
    slope = half + (half - half * half) * (act * (2.0 * root + 6.0 * cubic * square))
    return act * half, slope


def tick_kernel(height, step, sections, first, lead_ref, fresh_ref, relay_ref, weight_ref, coef_ref, point_ref, *rest):
    if not first:
        prev_ref, *rest = rest
    teach_ref, gel0, gel1, grad0, grad1, dk_ref, *rest = rest
    if sections:
        next_ref, *rest = rest
        *rest, land, send_sem, recv_sem = rest
        spot = lax.axis_index("section")
        later, earlier = lax.rem(spot + 1, sections), lax.rem(spot + sections - 1, sections)
        barrier = pltpu.get_barrier_semaphore()

        @pl.when(spot > 0)
        def _():
            pl.semaphore_signal(barrier, inc=1, device_id={"section": earlier}, device_id_type=MESH)

        copy = pltpu.make_async_remote_copy(
            src_ref=teach_ref,
            dst_ref=land,
            send_sem=send_sem,
            recv_sem=recv_sem,
            device_id={"section": later},
            device_id_type=MESH,
        )
    pad, hpad, src0, src1, src2, hid, slope0, slope1, dact0, cur_ref, u_one_ref, resid_ref, acc1, acc2 = rest
    gels, grads = (gel0, gel1), (grad0, grad1)
    srcs, slopes = (src0, src1), (slope0, slope1)
    rows, chans = cur_ref.shape
    blocks = chans // LANES
    pair = 2 * height
    units = rows // pair
    chunks = units // step
    pads = pad.shape[1]

    def span(index):
        return pl.ds(pl.multiple_of(index * step * pair, step * pair), step * pair)

    zero = jnp.zeros((height, LANES), F32)
    for block in range(blocks):
        for at in range(0, pads, pair):
            pad[block, at : at + height] = zero
            hpad[block, at : at + height] = zero

    lead = lead_ref[0] == 1
    current = jnp.where(lead, fresh_ref[...].astype(F32), relay_ref[...].astype(F32))
    cur_ref[...] = current
    put_padded(current, pad, height)
    spread(pad, src0, height, units, 3)
    acc1[...] = jnp.zeros_like(acc1)
    acc2[...] = jnp.zeros_like(acc2)

    def teach_chunk(at, src_ref, middle, which, acc):
        down, index = at // chunks, lax.rem(at, chunks)
        parts = []
        for right in range(3):
            start = index * step + middle - 1 + right
            for block in range(blocks):
                part = src_ref[block, middle - 1 + down, pl.ds(start, step)]
                parts.append(part.reshape(step * pair, LANES))
        deep = 3 * chans
        weights = weight_ref[which, pl.ds(pl.multiple_of(down * deep, deep), deep)]
        acc[span(index)] += jnp.dot(jnp.concatenate(parts, axis=1), weights, preferred_element_type=F32)

    def forward(which, src_ref, middle, acc):
        def chunk(at, carry):
            block, index = at // chunks, lax.rem(at, chunks)
            act = tap_sum(srcs[which], block, coef_ref, which, index * step, step, False)
            teach_chunk(at, src_ref, middle, which, acc)
            gel, slope = gelu_pair(act.reshape(step * pair, LANES))
            slopes[which][span(index), columns(block)] = slope
            gels[which][span(index), columns(block)] = gel.astype(BF16)
            return carry

        lax.fori_loop(0, blocks * chunks, chunk, 0)
        return jnp.dot(gels[which][...], point_ref[which], preferred_element_type=F32)

    u_one = forward(0, src0, 3, acc1) + cur_ref[...]
    u_one_ref[...] = u_one
    put_padded(u_one, pad, height)
    put_padded(jnp.maximum(acc1[...], 0.0), hpad, height)
    spread(hpad, hid, height, units, 1)
    spread(pad, src1, height, units, 3)

    diff = forward(1, hid, 1, acc2) + u_one_ref[...]
    teach = (0.8 * (cur_ref[...] + acc2[...])).astype(BF16)
    teach_ref[...] = teach
    resid = (diff - teach.astype(F32)) * (4.0 / rows)
    resid_ref[...] = resid
    grad1[...] = resid.astype(BF16)

    def back_point(which):
        dgel = lax.dot_general(grads[which][...], point_ref[which], NT, preferred_element_type=F32)
        return dgel * slopes[which][...]

    put_padded(back_point(1), pad, height)
    if sections:

        @pl.when(spot < sections - 1)
        def _():
            pl.semaphore_wait(barrier, 1)
            copy.start()

    spread(pad, src2, height, units, 3)

    def chunk_back(at, carry):
        block, index = at // chunks, lax.rem(at, chunks)
        back = tap_sum(src2, block, coef_ref, 1, index * step, step, True)
        back = back.reshape(step * pair, LANES) + resid_ref[span(index), columns(block)]
        grad0[span(index), columns(block)] = back.astype(BF16)
        return carry

    lax.fori_loop(0, blocks * chunks, chunk_back, 0)

    def taps_grad(which, part_of):
        def over_rows(row, carry):
            for block in range(blocks):
                strip = srcs[which][block, row]
                part = part_of(block)
                for col in range(7):
                    prod = strip[col : col + units] * part
                    size = units
                    while size > 1:
                        size //= 2
                        prod = prod[:size] + prod[size:]
                    wide = prod[0].astype(F32)
                    total = wide[:height] + wide[height:]
                    if not first:
                        total = total + prev_ref[which, block, row, col]
                    dk_ref[which, block, row, col] = total
            return carry

        lax.fori_loop(0, 7, over_rows, 0)

    taps_grad(1, lambda block: src2[block, 3, 3 : 3 + units])
    dact = back_point(0)
    for block in range(blocks):
        dact0[block] = dact[:, lanes(block)].reshape(units, pair, LANES).astype(BF16)
    taps_grad(0, lambda block: dact0[block])
    if sections:

        @pl.when(spot > 0)
        def _():
            copy.wait_recv()
            next_ref[...] = land[...]

        @pl.when(spot == 0)
        def _():
            next_ref[...] = jnp.zeros_like(next_ref)

        @pl.when(spot < sections - 1)
        def _():
            copy.wait_send()


def tick_call(lead, fresh, relay, weight, coef, point, prev, height, sections):
    rows, chans = fresh.shape
    blocks = chans // LANES
    pair = 2 * height
    units = rows // pair
    vmem = pl.BlockSpec(memory_space=pltpu.VMEM)
    flat = jax.ShapeDtypeStruct((rows, chans), BF16)
    outs = [flat] * 5 + [jax.ShapeDtypeStruct((2, blocks, 7, 7, height, LANES), F32)]
    pad_shape = pltpu.VMEM((blocks, (2 * 2 * units + 1) * height, LANES), F32)
    src_shape = pltpu.VMEM((blocks, 7, units + 6, pair, LANES), BF16)
    map_shape = pltpu.VMEM((rows, chans), F32)
    scratch = [pad_shape] * 2 + [src_shape] * 3
    scratch += [pltpu.VMEM((blocks, 3, units + 2, pair, LANES), BF16)]
    scratch += [map_shape] * 2 + [pltpu.VMEM((blocks, units, pair, LANES), BF16)] + [map_shape] * 5
    params = {}
    if sections:
        outs.append(flat)
        scratch += [pltpu.VMEM((rows, chans), BF16), pltpu.SemaphoreType.DMA, pltpu.SemaphoreType.DMA]
        params = {"collective_id": 0 if prev is None else 1, "has_side_effects": True}
    args = [lead, fresh, relay, weight, coef, point] + ([] if prev is None else [prev])
    return pl.pallas_call(
        functools.partial(tick_kernel, height, units // 2, sections, prev is None),
        out_shape=tuple(outs),
        in_specs=[pl.BlockSpec(memory_space=pltpu.SMEM)] + [vmem] * (len(args) - 1),
        out_specs=(vmem,) * len(outs),
        scratch_shapes=scratch,
        compiler_params=pltpu.CompilerParams(vmem_limit_bytes=24 << 20, **params),
        cost_estimate=pl.CostEstimate(
            flops=10_000_000_000, bytes_accessed=8 * rows * chans, transcendentals=0
        ),
        name="tick",
    )(*args)


def body(pipe_maps, fresh_maps, teacher_weight, student_depth, student_point):
    _, _, height, width, chans = pipe_maps.shape
    rows = height * width
    blocks = chans // LANES
    lead = (lax.axis_index("section") == 0).astype(jnp.int32).reshape(1)
    sections = lax.axis_size("section")

    def to_rows(maps):
        front = maps.shape[:-3]
        split = maps.reshape(front + (height, 2, width // 2, chans))
        return jnp.swapaxes(split, -4, -2).reshape(front + (rows, chans))

    relay = to_rows(pipe_maps[0, 0])
    fresh = to_rows(fresh_maps[:, 0])
    weight = teacher_weight.reshape(2, 9 * chans, chans)
    coef = student_depth.astype(BF16).reshape(2, 49, blocks, 1, LANES).swapaxes(1, 2)
    coef = jnp.broadcast_to(coef, (2, blocks, 49, 2 * height, LANES))
    ticks = fresh_maps.shape[0] + 1
    gels, grads, depth_total = [], [], None
    teach = relay
    for tick in range(ticks):
        mine = relay if tick == 0 else fresh[tick - 1]
        linked = sections if tick + 1 < ticks else 0
        teach, gel0, gel1, grad0, grad1, depth_total, *sent = tick_call(
            lead, mine, relay, weight, coef, student_point, depth_total, height, linked
        )
        if sent:
            relay = sent[0]
        gels.append((gel0, gel1))
        grads.append((grad0, grad1))
    gel_all = [jnp.concatenate([pair[b] for pair in gels]) for b in range(2)]
    grad_all = [jnp.concatenate([pair[b] for pair in grads]) for b in range(2)]
    point_total = [
        lax.dot_general(grad_all[b], gel_all[b], (((0,), (0,)), ((), ())), preferred_element_type=F32)
        for b in range(2)
    ]
    depth_rows = depth_total.sum(axis=4).transpose(1, 4, 0, 2, 3).reshape(chans, 98)
    packed = jnp.concatenate(point_total + [depth_rows], axis=1)
    parties = lax.axis_size("dp")
    share = chans // parties
    me = lax.axis_index("dp")
    total = lax.dynamic_slice_in_dim(packed, me * share, share, 0)
    for hop in range(1, parties):
        out = lax.dynamic_slice_in_dim(packed, lax.rem(me + hop, parties) * share, share, 0)
        pairs = [(i, (i + hop) % parties) for i in range(parties)]
        total = total + lax.ppermute(out.astype(BF16), "dp", pairs).astype(F32)
    point_grad = jnp.stack([total[:, b * chans : (b + 1) * chans] for b in range(2)]).swapaxes(1, 2)
    depth_grad = total[:, 2 * chans :].T.reshape(2, 49, share)
    final = jnp.swapaxes(teach.reshape(width // 2, 2, height, chans), 0, 2)
    final = final.reshape(1, 1, height, width, chans)
    return final, point_grad, depth_grad


def solution(mesh):
    placed = (
        P("section", "dp", None, None, None),
        P(None, "dp", None, None, None),
        P("section", None, None, None, None),
        P("section", None, None),
        P("section", None, None),
    )
    return jax.shard_map(
        body,
        mesh=mesh,
        in_specs=placed,
        out_specs=(
            P("section", "dp", None, None, None),
            P("section", None, "dp"),
            P("section", None, "dp"),
        ),
        check_vma=False,
    )
```

```python
import functools

import jax
import jax.numpy as jnp
from jax import lax
from jax.experimental import pallas as pl
from jax.experimental.pallas import tpu as pltpu
from jax.sharding import PartitionSpec as P

LANES = 128
F32 = jnp.float32
BF16 = jnp.bfloat16
MESH = pl.DeviceIdType.MESH
NT = (((1,), (1,)), ((), ()))


def lanes(block):
    return slice(block * LANES, (block + 1) * LANES)


def columns(block):
    return pl.ds(pl.multiple_of(block * LANES, LANES), LANES)


def put_padded(vals, pad_ref, height):
    units = vals.shape[0] // (2 * height)
    for block in range(vals.shape[1] // LANES):
        for unit in range(units):
            for half in range(2):
                at = (2 * unit + half) * height
                to = (2 * (unit + half * units) + 1) * height
                pad_ref[block, to : to + height] = vals[at : at + height, lanes(block)]


def spread(pad_ref, put, height, units, reach):
    def one_row(row, carry):
        for block in range(pad_ref.shape[0]):

            def load(w):
                return pad_ref[block, pl.ds((2 * w + 1) * height + row - reach, height)]

            zero = jnp.zeros((height, LANES), F32)
            cols = [load(w) for w in range(2 * units)]
            low = [zero] * reach + cols[: units + reach]
            high = cols[units - reach :] + [zero] * reach
            for unit in range(units + 2 * reach):
                put(block, row, unit, low[unit], high[unit])
        return carry

    lax.fori_loop(0, 2 * reach + 1, one_row, 0)


def strips(out_ref):
    def put(block, row, unit, low, high):
        out_ref[block, row, unit] = jnp.concatenate([low, high], axis=1).astype(BF16)

    return put


def windows(out_ref, height):
    def put(block, row, unit, low, high):
        at = slice(unit * 2 * height, (unit + 1) * 2 * height)
        out_ref[row, at, lanes(block)] = jnp.concatenate([low, high], axis=0).astype(BF16)

    return put


def beside(vals, height):
    split = vals.reshape(-1, 2 * height, LANES)
    return jnp.concatenate([split[:, :height], split[:, height:]], axis=2)


def below(vals, height):
    return jnp.concatenate([vals[:, :, :LANES], vals[:, :, LANES:]], axis=1).reshape(-1, LANES)


def tap_sum(src_ref, block, coef_ref, which, start, count, flip):
    total = None
    for rows in ((0, 1, 2, 3), (4, 5, 6)):
        part = None
        for row in rows:
            strip = src_ref[block, row, pl.ds(start, count + 6)]
            acc = None
            for col in range(7):
                tap = row * 7 + col
                tap = 48 - tap if flip else tap
                term = strip[col : col + count] * coef_ref[which, block, tap][None]
                acc = term if acc is None else acc + term
            part = acc if part is None else part + acc
        wide = part.astype(F32)
        total = wide if total is None else total + wide
    return total


def gelu_pair(act):
    root = 0.7978845608028654
    cubic = root * 0.044715
    square = act * act
    tanh = jnp.tanh(act * (root + cubic * square))
    half = 0.5 + 0.5 * tanh
    slope = half + (half - half * half) * (act * (2.0 * root + 6.0 * cubic * square))
    return act * half, slope


def tick_kernel(height, step, sections, first, lead_ref, fresh_ref, relay_ref, weight_ref, coef_ref, point_ref, *rest):
    if not first:
        prev_ref, *rest = rest
    teach_ref, gel0, gel1, grad0, grad1, dk_ref, *rest = rest
    if sections:
        next_ref, *rest = rest
        *rest, land, send_sem, recv_sem = rest
        spot = lax.axis_index("section")
        later, earlier = lax.rem(spot + 1, sections), lax.rem(spot + sections - 1, sections)
        barrier = pltpu.get_barrier_semaphore()

        @pl.when(spot > 0)
        def _():
            pl.semaphore_signal(barrier, inc=1, device_id={"section": earlier}, device_id_type=MESH)

        copy = pltpu.make_async_remote_copy(
            src_ref=teach_ref,
            dst_ref=land,
            send_sem=send_sem,
            recv_sem=recv_sem,
            device_id={"section": later},
            device_id_type=MESH,
        )
    pad, hpad, src0, src1, src2, win, slope0, slope1, dact0, cur_ref, u_one_ref, resid_ref, acc1, acc2 = rest
    gels, grads = (gel0, gel1), (grad0, grad1)
    srcs, slopes = (src0, src1), (slope0, slope1)
    rows, chans = cur_ref.shape
    blocks = chans // LANES
    pair = 2 * height
    units = rows // pair
    chunks = units // step
    pads = pad.shape[1]

    def span(index):
        return pl.ds(pl.multiple_of(index * step * pair, step * pair), step * pair)

    zero = jnp.zeros((height, LANES), F32)
    for block in range(blocks):
        for at in range(0, pads, pair):
            pad[block, at : at + height] = zero
            hpad[block, at : at + height] = zero

    lead = lead_ref[0] == 1
    current = jnp.where(lead, fresh_ref[...].astype(F32), relay_ref[...].astype(F32))
    cur_ref[...] = current
    put_padded(current, pad, height)
    spread(pad, windows(win, height), height, units, 1)
    spread(pad, strips(src0), height, units, 3)
    acc1[...] = jnp.zeros_like(acc1)
    acc2[...] = jnp.zeros_like(acc2)

    def teach_chunk(at, which, acc):
        down, index = at // chunks, lax.rem(at, chunks)
        parts = []
        for right in range(3):
            start = pl.multiple_of((index * step + right) * pair, pair)
            parts.append(win[down, pl.ds(start, step * pair)])
        deep = 3 * chans
        weights = weight_ref[which, pl.ds(pl.multiple_of(down * deep, deep), deep)]
        acc[span(index)] += jnp.dot(jnp.concatenate(parts, axis=1), weights, preferred_element_type=F32)

    def forward(which, acc):
        def chunk(at, carry):
            block, index = at // chunks, lax.rem(at, chunks)
            act = tap_sum(srcs[which], block, coef_ref, which, index * step, step, False)
            teach_chunk(at, which, acc)
            gel, slope = gelu_pair(below(act, height))
            slopes[which][span(index), columns(block)] = slope
            gels[which][span(index), columns(block)] = gel.astype(BF16)
            return carry

        lax.fori_loop(0, blocks * chunks, chunk, 0, unroll=blocks)
        return jnp.dot(gels[which][...], point_ref[which], preferred_element_type=F32)

    u_one = forward(0, acc1) + cur_ref[...]
    u_one_ref[...] = u_one
    put_padded(u_one, pad, height)
    put_padded(jnp.maximum(acc1[...], 0.0), hpad, height)
    spread(hpad, windows(win, height), height, units, 1)
    spread(pad, strips(src1), height, units, 3)

    diff = forward(1, acc2) + u_one_ref[...]
    teach = (0.8 * (cur_ref[...] + acc2[...])).astype(BF16)
    teach_ref[...] = teach
    resid = (diff - teach.astype(F32)) * (4.0 / rows)
    resid_ref[...] = resid
    grad1[...] = resid.astype(BF16)

    def back_point(which):
        dgel = lax.dot_general(grads[which][...], point_ref[which], NT, preferred_element_type=F32)
        return dgel * slopes[which][...]

    put_padded(back_point(1), pad, height)
    if sections:

        @pl.when(spot < sections - 1)
        def _():
            pl.semaphore_wait(barrier, 1)
            copy.start()

    spread(pad, strips(src2), height, units, 3)

    def chunk_back(at, carry):
        block, index = at // chunks, lax.rem(at, chunks)
        back = tap_sum(src2, block, coef_ref, 1, index * step, step, True)
        back = below(back, height) + resid_ref[span(index), columns(block)]
        grad0[span(index), columns(block)] = back.astype(BF16)
        return carry

    lax.fori_loop(0, blocks * chunks, chunk_back, 0)

    def taps_grad(which, part_of):
        for block in range(blocks):

            def over_rows(row, carry):
                strip = srcs[which][block, row]
                part = part_of(block)
                for col in range(7):
                    prod = strip[col : col + units] * part
                    size = units
                    while size > 1:
                        size //= 2
                        prod = prod[:size] + prod[size:]
                    wide = prod[0].astype(F32)
                    total = wide[:, :LANES] + wide[:, LANES:]
                    if not first:
                        total = total + prev_ref[which, block, row, col]
                    dk_ref[which, block, row, col] = total
                return carry

            lax.fori_loop(0, 7, over_rows, 0)

    taps_grad(1, lambda block: src2[block, 3, 3 : 3 + units])
    dact = back_point(0)
    for block in range(blocks):
        dact0[block] = beside(dact[:, lanes(block)], height).astype(BF16)
    taps_grad(0, lambda block: dact0[block])
    if sections:

        @pl.when(spot > 0)
        def _():
            copy.wait_recv()
            next_ref[...] = land[...]

        @pl.when(spot == 0)
        def _():
            next_ref[...] = jnp.zeros_like(next_ref)

        @pl.when(spot < sections - 1)
        def _():
            copy.wait_send()


def tick_call(lead, fresh, relay, weight, coef, point, prev, height, sections):
    rows, chans = fresh.shape
    blocks = chans // LANES
    pair = 2 * height
    units = rows // pair
    vmem = pl.BlockSpec(memory_space=pltpu.VMEM)
    flat = jax.ShapeDtypeStruct((rows, chans), BF16)
    outs = [flat] * 5 + [jax.ShapeDtypeStruct((2, blocks, 7, 7, height, LANES), F32)]
    pad_shape = pltpu.VMEM((blocks, (2 * 2 * units + 1) * height, LANES), F32)
    src_shape = pltpu.VMEM((blocks, 7, units + 6, height, 2 * LANES), BF16)
    map_shape = pltpu.VMEM((rows, chans), F32)
    scratch = [pad_shape] * 2 + [src_shape] * 3
    scratch += [pltpu.VMEM((3, (units + 2) * pair, chans), BF16)]
    scratch += [map_shape] * 2 + [pltpu.VMEM((blocks, units, height, 2 * LANES), BF16)] + [map_shape] * 5
    params = {}
    if sections:
        outs.append(flat)
        scratch += [pltpu.VMEM((rows, chans), BF16), pltpu.SemaphoreType.DMA, pltpu.SemaphoreType.DMA]
        params = {"collective_id": 0 if prev is None else 1, "has_side_effects": True}
    args = [lead, fresh, relay, weight, coef, point] + ([] if prev is None else [prev])
    return pl.pallas_call(
        functools.partial(tick_kernel, height, units // 2, sections, prev is None),
        out_shape=tuple(outs),
        in_specs=[pl.BlockSpec(memory_space=pltpu.SMEM)] + [vmem] * (len(args) - 1),
        out_specs=(vmem,) * len(outs),
        scratch_shapes=scratch,
        compiler_params=pltpu.CompilerParams(vmem_limit_bytes=24 << 20, **params),
        cost_estimate=pl.CostEstimate(
            flops=10_000_000_000, bytes_accessed=8 * rows * chans, transcendentals=0
        ),
        name="tick",
    )(*args)


def body(pipe_maps, fresh_maps, teacher_weight, student_depth, student_point):
    _, _, height, width, chans = pipe_maps.shape
    rows = height * width
    blocks = chans // LANES
    lead = (lax.axis_index("section") == 0).astype(jnp.int32).reshape(1)
    sections = lax.axis_size("section")

    def to_rows(maps):
        front = maps.shape[:-3]
        split = maps.reshape(front + (height, 2, width // 2, chans))
        return jnp.swapaxes(split, -4, -2).reshape(front + (rows, chans))

    relay = to_rows(pipe_maps[0, 0])
    fresh = to_rows(fresh_maps[:, 0])
    weight = teacher_weight.reshape(2, 9 * chans, chans)
    coef = student_depth.astype(BF16).reshape(2, 49, blocks, 1, 1, LANES).swapaxes(1, 2)
    coef = jnp.broadcast_to(coef, (2, blocks, 49, height, 2, LANES)).reshape(2, blocks, 49, height, 2 * LANES)
    ticks = fresh_maps.shape[0] + 1
    gels, grads, depth_total = [], [], None
    teach = relay
    for tick in range(ticks):
        mine = relay if tick == 0 else fresh[tick - 1]
        linked = sections if tick + 1 < ticks else 0
        teach, gel0, gel1, grad0, grad1, depth_total, *sent = tick_call(
            lead, mine, relay, weight, coef, student_point, depth_total, height, linked
        )
        if sent:
            relay = sent[0]
        gels.append((gel0, gel1))
        grads.append((grad0, grad1))
    gel_all = [jnp.concatenate([pair[b] for pair in gels]) for b in range(2)]
    grad_all = [jnp.concatenate([pair[b] for pair in grads]) for b in range(2)]
    point_total = [
        lax.dot_general(grad_all[b], gel_all[b], (((0,), (0,)), ((), ())), preferred_element_type=F32)
        for b in range(2)
    ]
    depth_rows = depth_total.sum(axis=4).transpose(1, 4, 0, 2, 3).reshape(chans, 98)
    packed = jnp.concatenate(point_total + [depth_rows], axis=1)
    parties = lax.axis_size("dp")
    share = chans // parties
    me = lax.axis_index("dp")
    total = lax.dynamic_slice_in_dim(packed, me * share, share, 0)
    for hop in range(1, parties):
        out = lax.dynamic_slice_in_dim(packed, lax.rem(me + hop, parties) * share, share, 0)
        pairs = [(i, (i + hop) % parties) for i in range(parties)]
        total = total + lax.ppermute(out.astype(BF16), "dp", pairs).astype(F32)
    point_grad = jnp.stack([total[:, b * chans : (b + 1) * chans] for b in range(2)]).swapaxes(1, 2)
    depth_grad = total[:, 2 * chans :].T.reshape(2, 49, share)
    final = jnp.swapaxes(teach.reshape(width // 2, 2, height, chans), 0, 2)
    final = final.reshape(1, 1, height, width, chans)
    return final, point_grad, depth_grad


def solution(mesh):
    placed = (
        P("section", "dp", None, None, None),
        P(None, "dp", None, None, None),
        P("section", None, None, None, None),
        P("section", None, None),
        P("section", None, None),
    )
    return jax.shard_map(
        body,
        mesh=mesh,
        in_specs=placed,
        out_specs=(
            P("section", "dp", None, None, None),
            P("section", None, "dp"),
            P("section", None, "dp"),
        ),
        check_vma=False,
    )
```

```python
import functools

import jax
import jax.numpy as jnp
from jax import lax
from jax.experimental import pallas as pl
from jax.experimental.pallas import tpu as pltpu
from jax.sharding import PartitionSpec as P

LANES = 128
F32 = jnp.float32
BF16 = jnp.bfloat16
MESH = pl.DeviceIdType.MESH
NT = (((1,), (1,)), ((), ()))
TN = (((0,), (0,)), ((), ()))
SIDE = 7


def lanes(block):
    return slice(block * LANES, (block + 1) * LANES)


def columns(block):
    return pl.ds(pl.multiple_of(block * LANES, LANES), LANES)


def put_padded(vals, pad_ref, height):
    units = vals.shape[0] // (2 * height)
    for block in range(vals.shape[1] // LANES):
        for unit in range(units):
            for half in range(2):
                at = (2 * unit + half) * height
                to = (2 * (unit + half * units) + 1) * height
                pad_ref[block, to : to + height] = vals[at : at + height, lanes(block)]


def get_padded(pad_ref, block, height, units):
    rows = []
    for unit in range(units):
        for half in range(2):
            at = (2 * (unit + half * units) + 1) * height
            rows.append(pad_ref[block, at : at + height])
    return jnp.concatenate(rows, axis=0)


def spread(pad_ref, put, height, units, reach):
    def one_row(row, carry):
        for block in range(pad_ref.shape[0]):

            def load(w):
                return pad_ref[block, pl.ds((2 * w + 1) * height + row - reach, height)]

            zero = jnp.zeros((height, LANES), F32)
            cols = [load(w) for w in range(2 * units)]
            low = [zero] * reach + cols[: units + reach]
            high = cols[units - reach :] + [zero] * reach
            for unit in range(units + 2 * reach):
                put(block, row, unit, low[unit], high[unit])
        return carry

    lax.fori_loop(0, 2 * reach + 1, one_row, 0)


def strips(out_ref):
    def put(block, row, unit, low, high):
        out_ref[block, row, unit] = jnp.concatenate([low, high], axis=1).astype(BF16)

    return put


def windows(out_ref, height):
    def put(block, row, unit, low, high):
        at = slice(unit * 2 * height, (unit + 1) * 2 * height)
        out_ref[row, at, lanes(block)] = jnp.concatenate([low, high], axis=0).astype(BF16)

    return put


def beside(vals, height):
    split = vals.reshape(-1, 2 * height, LANES)
    return jnp.concatenate([split[:, :height], split[:, height:]], axis=2)


def below(vals):
    return jnp.concatenate([vals[:, :, :LANES], vals[:, :, LANES:]], axis=1).reshape(-1, LANES)


def tap_sum(src_ref, block, coef_ref, which, start, count, flip):
    total = None
    for rows in ((0, 1, 2, 3), (4, 5, 6)):
        part = None
        for row in rows:
            strip = src_ref[block, row, pl.ds(start, count + 6)]
            acc = None
            for col in range(SIDE):
                tap = row * SIDE + col
                tap = 48 - tap if flip else tap
                term = strip[col : col + count] * coef_ref[which, block, tap][None]
                acc = term if acc is None else acc + term
            part = acc if part is None else part + acc
        wide = part.astype(F32)
        total = wide if total is None else total + wide
    return total


def gelu_pair(act):
    root = 0.7978845608028654
    cubic = root * 0.044715
    square = act * act
    tanh = jnp.tanh(act * (root + cubic * square))
    half = 0.5 + 0.5 * tanh
    slope = half + (half - half * half) * (act * (2.0 * root + 6.0 * cubic * square))
    return act * half, slope


def step_kernel(
    height, step, ticks, sections, parties,
    pipe_hbm, fresh_hbm, weight_hbm, taps_ref, point_hbm,
    final_ref, pg_ref, pg_in_ref, dk_ref, dk_in_ref,
    raw, weight, point, raw_sem, weight_sem, point_sem,
    teach, land, send_sem, recv_sem,
    pg_out, pg_land, dk_out, dk_land, swap_send, swap_recv,
    coef, pad, hpad, src0, src1, src2, win, slope0, slope1, dact0, cur, u_one, resid, gels, grads, sums,
):
    rows, chans = cur.shape
    blocks = chans // LANES
    pair = 2 * height
    units = rows // pair
    chunks = units // step
    share = chans // parties
    srcs, slopes = (src0, src1), (slope0, slope1)
    spot, me = lax.axis_index("section"), lax.axis_index("dp")
    barrier = pltpu.get_barrier_semaphore()

    @pl.when(spot > 0)
    def _():
        pl.semaphore_signal(barrier, inc=1, device_id={"section": spot - 1}, device_id_type=MESH)

    for hop in range(1, parties):
        peer = lax.rem(me + hop, parties)
        pl.semaphore_signal(barrier, inc=1, device_id={"dp": peer}, device_id_type=MESH)

    fetch_pipe = pltpu.make_async_copy(pipe_hbm, raw.at[0], raw_sem.at[0])
    fetch_fresh = pltpu.make_async_copy(fresh_hbm, raw.at[pl.ds(1, ticks - 1)], raw_sem.at[1])
    fetch_weight = [pltpu.make_async_copy(weight_hbm.at[i], weight.at[i], weight_sem.at[i]) for i in range(2)]
    fetch_point = pltpu.make_async_copy(point_hbm, point, point_sem)
    for fetch in (fetch_pipe, fetch_weight[0], fetch_weight[1], fetch_point, fetch_fresh):
        fetch.start()

    def span(index):
        return pl.ds(pl.multiple_of(index * step * pair, step * pair), step * pair)

    zero = jnp.zeros((height, LANES), F32)
    for block in range(blocks):
        for at in range(0, pad.shape[1], pair):
            pad[block, at : at + height] = zero
            hpad[block, at : at + height] = zero
    for which in range(2):
        for block in range(blocks):
            for tap in range(SIDE * SIDE):
                line = jnp.broadcast_to(taps_ref[tap, which : which + 1, lanes(block)], (height, LANES))
                coef[which, block, tap] = jnp.concatenate([line, line], axis=1).astype(BF16)
    sums[...] = jnp.zeros_like(sums)

    def take_raw(tick):
        for row in range(height):
            line = raw[tick, row].astype(F32)
            for block in range(blocks):
                pad[block, pl.ds(height + row, 2 * units, stride=pair)] = line[:, lanes(block)]

    def keep_input():
        for block in range(blocks):
            cur[:, lanes(block)] = get_padded(pad, block, height, units)
        spread(pad, windows(win, height), height, units, 1)

    def conv(which):
        parts = [win[down, right * pair : right * pair + rows] for down in range(3) for right in range(3)]
        return jnp.dot(jnp.concatenate(parts, axis=1), weight[which], preferred_element_type=F32)

    def keep_hidden(hidden):
        put_padded(jnp.maximum(hidden, 0.0), hpad, height)
        spread(hpad, windows(win, height), height, units, 1)

    def keep_teach(second, tick):
        teach[tick] = (0.8 * (cur[...] + second)).astype(BF16)

    def relay(tick):
        return pltpu.make_async_remote_copy(
            src_ref=teach.at[tick],
            dst_ref=land.at[tick],
            send_sem=send_sem.at[tick],
            recv_sem=recv_sem.at[tick],
            device_id={"section": lax.rem(spot + 1, sections)},
            device_id_type=MESH,
        )

    def send(tick):
        @pl.when(spot < sections - 1)
        def _():
            relay(tick).start()

    def back_point(which, tick):
        dgel = lax.dot_general(grads[which, tick], point[which], NT, preferred_element_type=F32)
        return dgel * slopes[which][...]

    def forward(which, tick):
        def chunk(at, carry):
            block, index = at // chunks, lax.rem(at, chunks)
            act = tap_sum(srcs[which], block, coef, which, index * step, step, False)
            gel, slope = gelu_pair(below(act))
            slopes[which][span(index), columns(block)] = slope
            gels[which, tick, span(index), columns(block)] = gel.astype(BF16)
            return carry

        lax.fori_loop(0, blocks * chunks, chunk, 0)
        return jnp.dot(gels[which, tick], point[which], preferred_element_type=F32)

    def student(tick):
        spread(pad, strips(src0), height, units, 3)
        middle = forward(0, tick) + cur[...]
        u_one[...] = middle
        put_padded(middle, pad, height)
        spread(pad, strips(src1), height, units, 3)
        diff = forward(1, tick) + u_one[...] - teach[tick].astype(F32)
        left = diff * (4.0 / rows)
        resid[...] = left
        grads[1, tick] = left.astype(BF16)
        put_padded(back_point(1, tick), pad, height)
        spread(pad, strips(src2), height, units, 3)

        def chunk_back(at, carry):
            block, index = at // chunks, lax.rem(at, chunks)
            back = tap_sum(src2, block, coef, 1, index * step, step, True)
            back = below(back) + resid[span(index), columns(block)]
            grads[0, tick, span(index), columns(block)] = back.astype(BF16)
            return carry

        lax.fori_loop(0, blocks * chunks, chunk_back, 0)
        dact = back_point(0, tick)
        for block in range(blocks):
            dact0[block] = beside(dact[:, lanes(block)], height).astype(BF16)

    def taps_grad(which):
        for block in range(blocks):
            part = src2[block, 3, 3 : 3 + units] if which else dact0[block]
            for row in range(SIDE):
                strip = srcs[which][block, row]
                for col in range(SIDE):
                    prod = strip[col : col + units] * part
                    size = units
                    while size > 1:
                        size //= 2
                        prod = prod[:size] + prod[size:]
                    wide = prod[0].astype(F32)
                    sums[which, block, row, col] += wide[:, :LANES] + wide[:, LANES:]

    fetch_pipe.wait()
    take_raw(0)
    keep_input()
    fetch_weight[0].wait()
    keep_hidden(conv(0))
    fetch_weight[1].wait()
    keep_teach(conv(1), 0)
    pl.semaphore_wait(barrier, parties - 1 + (spot < sections - 1).astype(jnp.int32))
    send(0)
    fetch_point.wait()
    fetch_fresh.wait()

    def tick_body(tick, carry):
        student(tick)

        @pl.when(spot > 0)
        def _():
            relay(tick).wait_recv()
            put_padded(land[tick].astype(F32), pad, height)

        @pl.when(spot == 0)
        def _():
            take_raw(tick + 1)

        keep_input()
        hidden = conv(0)
        taps_grad(1)
        keep_hidden(hidden)
        second = conv(1)
        taps_grad(0)
        keep_teach(second, tick + 1)

        @pl.when(tick + 1 < ticks - 1)
        def _():
            send(tick + 1)

        return carry

    lax.fori_loop(0, ticks - 1, tick_body, 0)
    last = ticks - 1
    for block in range(blocks):
        hpad_rows = teach[last, :, lanes(block)].astype(F32)
        for unit in range(units):
            for half in range(2):
                at = (2 * unit + half) * height
                to = (2 * (unit + half * units) + 1) * height
                hpad[block, to : to + height] = hpad_rows[at : at + height]
    for row in range(height):
        parts = [hpad[block, pl.ds(height + row, 2 * units, stride=pair)] for block in range(blocks)]
        final_ref[row] = jnp.concatenate(parts, axis=1).astype(BF16)
    student(last)

    def swap(hop, which):
        src, dst = (dk_out, dk_land.at[hop - 1]) if which == 2 else (None, None)
        peer = lax.rem(me + hop, parties)
        if src is None:
            src = pg_out.at[which, pl.ds(pl.multiple_of(peer * share, 16), share)]
            dst = pg_land.at[hop - 1, which]
        return pltpu.make_async_remote_copy(
            src_ref=src,
            dst_ref=dst,
            send_sem=swap_send.at[hop - 1, which],
            recv_sem=swap_recv.at[hop - 1, which],
            device_id={"dp": peer},
            device_id_type=MESH,
        )

    def point_grad(which):
        up = grads[which].reshape(ticks * rows, chans)
        total = lax.dot_general(up, gels[which].reshape(ticks * rows, chans), TN, preferred_element_type=F32)
        pg_ref[which] = total
        pg_out[which] = total.astype(BF16)

    point_grad(1)
    taps_grad(1)
    for hop in range(1, parties):
        swap(hop, 1).start()
    point_grad(0)
    taps_grad(0)
    for hop in range(1, parties):
        swap(hop, 0).start()
    for which in range(2):
        for block in range(blocks):
            for row in range(SIDE):
                line = jnp.sum(sums[which, block, row], axis=1)
                at = slice(row * SIDE, (row + 1) * SIDE)
                dk_ref[which, at, lanes(block)] = line
    dk_out[...] = dk_ref[...].astype(BF16)
    for hop in range(1, parties):
        swap(hop, 2).start()
    for which in (1, 0, 2):
        for hop in range(1, parties):
            swap(hop, which).wait_recv()
    pg_in_ref[...] = pg_land[...]
    dk_in_ref[...] = dk_land[...]
    for which in (1, 0, 2):
        for hop in range(1, parties):
            swap(hop, which).wait_send()

    @pl.when(spot < sections - 1)
    def _():
        for tick in range(ticks - 1):
            relay(tick).wait_send()


def finish_kernel(parties, final_in, pg_ref, pg_in_ref, dk_ref, dk_in_ref, final_ref, point_ref, depth_ref):
    me = lax.axis_index("dp")
    share = point_ref.shape[1]
    final_ref[...] = final_in[...]
    for which in range(2):
        total = pg_ref[which, pl.ds(pl.multiple_of(me * share, 16), share)]
        for hop in range(parties - 1):
            total = total + pg_in_ref[hop, which].astype(F32)
        point_ref[which] = total
        depth = dk_ref[which]
        for hop in range(parties - 1):
            depth = depth + dk_in_ref[hop, which].astype(F32)
        for party in range(parties):

            @pl.when(me == party)
            def _():
                depth_ref[which] = depth[:, party * share : (party + 1) * share]


def body(pipe_maps, fresh_maps, teacher_weight, student_depth, student_point):
    _, _, height, width, chans = pipe_maps.shape
    rows = height * width
    blocks = chans // LANES
    pair = 2 * height
    units = rows // pair
    ticks = fresh_maps.shape[0] + 1
    sections, parties = lax.axis_size("section"), lax.axis_size("dp")
    share = chans // parties
    peers = max(parties - 1, 1)
    hbm = pl.BlockSpec(memory_space=pl.ANY)
    vmem = pl.BlockSpec(memory_space=pltpu.VMEM)
    dma = pltpu.SemaphoreType.DMA
    pad_shape = pltpu.VMEM((blocks, (2 * width + 1) * height, LANES), F32)
    src_shape = pltpu.VMEM((blocks, SIDE, units + 6, height, 2 * LANES), BF16)
    map_shape = pltpu.VMEM((rows, chans), F32)
    taps = SIDE * SIDE
    results = (
        jax.ShapeDtypeStruct((height, width, chans), BF16),
        jax.ShapeDtypeStruct((2, chans, chans), F32),
        jax.ShapeDtypeStruct((peers, 2, share, chans), BF16),
        jax.ShapeDtypeStruct((2, taps, chans), F32),
        jax.ShapeDtypeStruct((peers, 2, taps, chans), BF16),
    )
    outs = pl.pallas_call(
        functools.partial(step_kernel, height, units // 2, ticks, sections, parties),
        out_shape=results,
        in_specs=[hbm, hbm, hbm, vmem, hbm],
        out_specs=(vmem,) * len(results),
        scratch_shapes=[
            pltpu.VMEM((ticks, height, width, chans), BF16),
            pltpu.VMEM((2, 9 * chans, chans), BF16),
            pltpu.VMEM((2, chans, chans), BF16),
            dma((2,)),
            dma((2,)),
            dma,
            pltpu.VMEM((ticks, rows, chans), BF16),
            pltpu.VMEM((ticks - 1, rows, chans), BF16),
            dma((ticks - 1,)),
            dma((ticks - 1,)),
            pltpu.VMEM((2, chans, chans), BF16),
            pltpu.VMEM((peers, 2, share, chans), BF16),
            pltpu.VMEM((2, taps, chans), BF16),
            pltpu.VMEM((peers, 2, taps, chans), BF16),
            dma((peers, 3)),
            dma((peers, 3)),
            pltpu.VMEM((2, blocks, taps, height, 2 * LANES), BF16),
            pad_shape,
            pad_shape,
            src_shape,
            src_shape,
            src_shape,
            pltpu.VMEM((3, (units + 2) * pair, chans), BF16),
            map_shape,
            map_shape,
            pltpu.VMEM((blocks, units, height, 2 * LANES), BF16),
            map_shape,
            map_shape,
            map_shape,
            pltpu.VMEM((2, ticks, rows, chans), BF16),
            pltpu.VMEM((2, ticks, rows, chans), BF16),
            pltpu.VMEM((2, blocks, SIDE, SIDE, height, LANES), F32),
        ],
        compiler_params=pltpu.CompilerParams(
            vmem_limit_bytes=44 << 20, collective_id=0, has_side_effects=True
        ),
        name="step",
    )(
        pipe_maps[0, 0],
        fresh_maps[:, 0],
        teacher_weight.reshape(2, 9 * chans, chans),
        student_depth.swapaxes(0, 1),
        student_point,
    )
    final, point_grad, depth_grad = pl.pallas_call(
        functools.partial(finish_kernel, parties),
        out_shape=(
            results[0],
            jax.ShapeDtypeStruct((2, share, chans), F32),
            jax.ShapeDtypeStruct((2, taps, share), F32),
        ),
        in_specs=[vmem] * len(outs),
        out_specs=(vmem,) * 3,
        name="finish",
    )(*outs)
    return final[None, None], point_grad.swapaxes(1, 2), depth_grad


def solution(mesh):
    placed = (
        P("section", "dp", None, None, None),
        P(None, "dp", None, None, None),
        P("section", None, None, None, None),
        P("section", None, None),
        P("section", None, None),
    )
    return jax.shard_map(
        body,
        mesh=mesh,
        in_specs=placed,
        out_specs=(
            P("section", "dp", None, None, None),
            P("section", None, "dp"),
            P("section", None, "dp"),
        ),
        check_vma=False,
    )
```

```python
import functools

import jax
import jax.numpy as jnp
from jax import lax
from jax.experimental import pallas as pl
from jax.experimental.pallas import tpu as pltpu
from jax.sharding import PartitionSpec as P

LANES = 128
F32 = jnp.float32
BF16 = jnp.bfloat16
MESH = pl.DeviceIdType.MESH
NT = (((1,), (1,)), ((), ()))
TN = (((0,), (0,)), ((), ()))
SIDE = 7


def lanes(block):
    return slice(block * LANES, (block + 1) * LANES)


def columns(block):
    return pl.ds(pl.multiple_of(block * LANES, LANES), LANES)


def put_padded(vals, pad_ref, height, first=0):
    units = vals.shape[0] // (2 * height)
    for block in range(vals.shape[1] // LANES):
        for unit in range(units):
            for half in range(2):
                at = (2 * unit + half) * height
                to = (2 * (unit + half * units) + 1) * height
                pad_ref[first + block, to : to + height] = vals[at : at + height, lanes(block)]


def get_padded(pad_ref, block, height, units):
    rows = []
    for unit in range(units):
        for half in range(2):
            at = (2 * (unit + half * units) + 1) * height
            rows.append(pad_ref[block, at : at + height])
    return jnp.concatenate(rows, axis=0)


def spread(pad_ref, put, height, units, reach, group=None):
    def one_row(row, carry):
        for block in group or range(pad_ref.shape[0]):

            def load(w):
                return pad_ref[block, pl.ds((2 * w + 1) * height + row - reach, height)]

            zero = jnp.zeros((height, LANES), F32)
            cols = [load(w) for w in range(2 * units)]
            low = [zero] * reach + cols[: units + reach]
            high = cols[units - reach :] + [zero] * reach
            for unit in range(units + 2 * reach):
                put(block, row, unit, low[unit], high[unit])
        return carry

    lax.fori_loop(0, 2 * reach + 1, one_row, 0)


def strips(out_ref):
    def put(block, row, unit, low, high):
        out_ref[block, row, unit] = jnp.concatenate([low, high], axis=1).astype(BF16)

    return put


def windows(out_ref, height):
    def put(block, row, unit, low, high):
        at = slice(unit * 2 * height, (unit + 1) * 2 * height)
        out_ref[row, at, lanes(block)] = jnp.concatenate([low, high], axis=0).astype(BF16)

    return put


def beside(vals, height):
    split = vals.reshape(-1, 2 * height, LANES)
    return jnp.concatenate([split[:, :height], split[:, height:]], axis=2)


def below(vals):
    return jnp.concatenate([vals[:, :, :LANES], vals[:, :, LANES:]], axis=1).reshape(-1, LANES)


def tap_sum(src_ref, block, coef_ref, which, start, count, flip):
    total = None
    for rows in ((0, 1, 2, 3), (4, 5, 6)):
        part = None
        for row in rows:
            strip = src_ref[block, row, pl.ds(start, count + 6)]
            acc = None
            for col in range(SIDE):
                tap = row * SIDE + col
                tap = 48 - tap if flip else tap
                term = strip[col : col + count] * coef_ref[which, block, tap][None]
                acc = term if acc is None else acc + term
            part = acc if part is None else part + acc
        wide = part.astype(F32)
        total = wide if total is None else total + wide
    return total


def gelu_pair(act):
    root = 0.7978845608028654
    cubic = root * 0.044715
    square = act * act
    tanh = jnp.tanh(act * (root + cubic * square))
    half = 0.5 + 0.5 * tanh
    slope = half + (half - half * half) * (act * (2.0 * root + 6.0 * cubic * square))
    return act * half, slope


def step_kernel(
    height, step, ticks, sections, parties,
    pipe_hbm, fresh_hbm, weight_hbm, taps_ref, point_hbm,
    final_ref, pg_ref, pg_in_ref, dk_ref, dk_in_ref,
    raw, weight, point, raw_sem, weight_sem, point_sem,
    teach, land, send_sem, recv_sem,
    pg_out, pg_land, dk_out, dk_land, swap_send, swap_recv,
    coef, pad, hpad, src0, src1, src2, win, slope0, slope1, dact0, cur, acc, u_one, resid, gels, grads, sums,
):
    rows, chans = cur.shape
    blocks = chans // LANES
    pair = 2 * height
    units = rows // pair
    chunks = units // step
    share = chans // parties
    srcs, slopes = (src0, src1), (slope0, slope1)
    spot, me = lax.axis_index("section"), lax.axis_index("dp")
    barrier = pltpu.get_barrier_semaphore()

    @pl.when(spot > 0)
    def _():
        pl.semaphore_signal(barrier, inc=1, device_id={"section": spot - 1}, device_id_type=MESH)

    for hop in range(1, parties):
        peer = lax.rem(me + hop, parties)
        pl.semaphore_signal(barrier, inc=1, device_id={"dp": peer}, device_id_type=MESH)

    fetch_pipe = pltpu.make_async_copy(pipe_hbm, raw.at[0], raw_sem.at[0])
    fetch_fresh = pltpu.make_async_copy(fresh_hbm, raw.at[pl.ds(1, ticks - 1)], raw_sem.at[1])
    fetch_weight = [pltpu.make_async_copy(weight_hbm.at[i], weight.at[i], weight_sem.at[i]) for i in range(2)]
    fetch_point = pltpu.make_async_copy(point_hbm, point, point_sem)
    for fetch in (fetch_pipe, fetch_weight[0], fetch_weight[1], fetch_point, fetch_fresh):
        fetch.start()

    def span(index):
        return pl.ds(pl.multiple_of(index * step * pair, step * pair), step * pair)

    zero = jnp.zeros((height, LANES), F32)
    for block in range(blocks):
        for at in range(0, pad.shape[1], pair):
            pad[block, at : at + height] = zero
            hpad[block, at : at + height] = zero
    for which in range(2):
        for block in range(blocks):
            for tap in range(SIDE * SIDE):
                line = jnp.broadcast_to(taps_ref[tap, which : which + 1, lanes(block)], (height, LANES))
                coef[which, block, tap] = jnp.concatenate([line, line], axis=1).astype(BF16)
    sums[...] = jnp.zeros_like(sums)

    def take_raw(tick, group):
        for row in range(height):
            for block in group:
                line = raw[tick, row, :, lanes(block)].astype(F32)
                pad[block, pl.ds(height + row, 2 * units, stride=pair)] = line

    def keep_input(group):
        for block in group:
            cur[:, lanes(block)] = get_padded(pad, block, height, units)
        spread(pad, windows(win, height), height, units, 1, group)

    def half_rows(half):
        return slice(half * rows // 2, (half + 1) * rows // 2)

    def window(half, down, right, cols):
        start = right * pair + half * rows // 2
        return win[down, start : start + rows // 2, cols]

    def first_conv(block, half):
        spots = [(down, right) for down in range(3) for right in range(3)]
        left = jnp.concatenate([window(half, down, right, lanes(block)) for down, right in spots], axis=1)
        starts = [(3 * down + right) * chans + block * LANES for down, right in spots]
        deep = jnp.concatenate([weight[0, at : at + LANES] for at in starts], axis=0)
        part = jnp.dot(left, deep, preferred_element_type=F32)
        acc[half_rows(half)] = part if block == 0 else acc[half_rows(half)] + part

    def second_conv(cols, half, tick):
        spots = [(down, right) for down in range(3) for right in range(3)]
        left = jnp.concatenate([window(half, down, right, slice(None)) for down, right in spots], axis=1)
        part = jnp.dot(left, weight[1, :, cols], preferred_element_type=F32)
        teach[tick, half_rows(half), cols] = (0.8 * (cur[half_rows(half), cols] + part)).astype(BF16)

    def keep_hidden():
        put_padded(jnp.maximum(acc[...], 0.0), hpad, height)
        spread(hpad, windows(win, height), height, units, 1)

    early = list(range(max(1, 2 * blocks // 3)))
    groups = [early, [block for block in range(blocks) if block not in early]]
    groups = [group for group in groups if group]

    def group_columns(group):
        return slice(group[0] * LANES, (group[-1] + 1) * LANES)

    def relay(tick, part):
        cols = group_columns(groups[part])
        return pltpu.make_async_remote_copy(
            src_ref=teach.at[tick, :, cols],
            dst_ref=land.at[tick, :, cols],
            send_sem=send_sem.at[tick, part],
            recv_sem=recv_sem.at[tick, part],
            device_id={"section": lax.rem(spot + 1, sections)},
            device_id_type=MESH,
        )

    def send(tick, part):
        @pl.when(spot < sections - 1)
        def _():
            relay(tick, part).start()

    def mix(main, side):
        done = 0
        for at, step_of in enumerate(main):
            upto = len(side) * (at + 1) // len(main)
            for other in side[done:upto]:
                other()
            done = upto
            step_of()

    def run_first(part, side):
        main = [functools.partial(first_conv, block, half) for block in groups[part] for half in range(2)]
        mix(main, side)

    def run_second(part, tick, side):
        cols = group_columns(groups[part])
        mix([functools.partial(second_conv, cols, half, tick) for half in range(2)], side)

    def back_point(which, tick):
        dgel = lax.dot_general(grads[which, tick], point[which], NT, preferred_element_type=F32)
        return dgel * slopes[which][...]

    def forward(which, tick):
        def chunk(at, carry):
            block, index = at // chunks, lax.rem(at, chunks)
            act = tap_sum(srcs[which], block, coef, which, index * step, step, False)
            gel, slope = gelu_pair(below(act))
            slopes[which][span(index), columns(block)] = slope
            gels[which, tick, span(index), columns(block)] = gel.astype(BF16)
            return carry

        lax.fori_loop(0, blocks * chunks, chunk, 0)
        return jnp.dot(gels[which, tick], point[which], preferred_element_type=F32)

    def student(tick):
        spread(pad, strips(src0), height, units, 3)
        middle = forward(0, tick) + cur[...]
        u_one[...] = middle
        put_padded(middle, pad, height)
        spread(pad, strips(src1), height, units, 3)
        diff = forward(1, tick) + u_one[...] - teach[tick].astype(F32)
        left = diff * (4.0 / rows)
        resid[...] = left
        grads[1, tick] = left.astype(BF16)
        put_padded(back_point(1, tick), pad, height)
        spread(pad, strips(src2), height, units, 3)

        def chunk_back(at, carry):
            block, index = at // chunks, lax.rem(at, chunks)
            back = tap_sum(src2, block, coef, 1, index * step, step, True)
            back = below(back) + resid[span(index), columns(block)]
            grads[0, tick, span(index), columns(block)] = back.astype(BF16)
            return carry

        lax.fori_loop(0, blocks * chunks, chunk_back, 0)
        dact = back_point(0, tick)
        for block in range(blocks):
            dact0[block] = beside(dact[:, lanes(block)], height).astype(BF16)

    def tap_row(which, block, row):
        part = src2[block, 3, 3 : 3 + units] if which else dact0[block]
        strip = srcs[which][block, row]
        for col in range(SIDE):
            prod = strip[col : col + units] * part
            size = units
            while size > 1:
                size //= 2
                prod = prod[:size] + prod[size:]
            wide = prod[0].astype(F32)
            sums[which, block, row, col] += wide[:, :LANES] + wide[:, LANES:]

    def tap_rows(which):
        return [functools.partial(tap_row, which, block, row) for block in range(blocks) for row in range(SIDE)]

    def share_out(steps):
        cut = [0]
        for group in groups:
            cut.append(cut[-1] + len(group) * len(steps) // blocks)
        return [steps[cut[i] : cut[i + 1]] for i in range(len(groups))]

    fetch_pipe.wait()
    take_raw(0, range(blocks))
    keep_input(range(blocks))
    fetch_weight[0].wait()
    for part in range(len(groups)):
        run_first(part, [])
    keep_hidden()
    fetch_weight[1].wait()
    pl.semaphore_wait(barrier, parties - 1 + (spot < sections - 1).astype(jnp.int32))
    for part in range(len(groups)):
        run_second(part, 0, [])
        send(0, part)
    fetch_point.wait()
    fetch_fresh.wait()

    def tick_body(tick, carry):
        student(tick)
        sides = share_out(tap_rows(1))
        for part, group in enumerate(groups):

            @pl.when(spot > 0)
            def _():
                relay(tick, part).wait_recv()
                put_padded(land[tick, :, group_columns(group)].astype(F32), pad, height, group[0])

            @pl.when(spot == 0)
            def _():
                take_raw(tick + 1, group)

            keep_input(group)
            run_first(part, sides[part])
        keep_hidden()
        steps = tap_rows(0)
        for part in range(len(groups)):
            many = len(steps) // len(groups)
            run_second(part, tick + 1, steps[part * many : (part + 1) * many if part + 1 < len(groups) else len(steps)])

            @pl.when(tick + 1 < ticks - 1)
            def _():
                send(tick + 1, part)

        return carry

    lax.fori_loop(0, ticks - 1, tick_body, 0)
    last = ticks - 1
    for block in range(blocks):
        hpad_rows = teach[last, :, lanes(block)].astype(F32)
        for unit in range(units):
            for half in range(2):
                at = (2 * unit + half) * height
                to = (2 * (unit + half * units) + 1) * height
                hpad[block, to : to + height] = hpad_rows[at : at + height]
    for row in range(height):
        parts = [hpad[block, pl.ds(height + row, 2 * units, stride=pair)] for block in range(blocks)]
        final_ref[row] = jnp.concatenate(parts, axis=1).astype(BF16)
    student(last)

    def swap(hop, which):
        src, dst = (dk_out, dk_land.at[hop - 1]) if which == 2 else (None, None)
        peer = lax.rem(me + hop, parties)
        if src is None:
            src = pg_out.at[which, pl.ds(pl.multiple_of(peer * share, 16), share)]
            dst = pg_land.at[hop - 1, which]
        return pltpu.make_async_remote_copy(
            src_ref=src,
            dst_ref=dst,
            send_sem=swap_send.at[hop - 1, which],
            recv_sem=swap_recv.at[hop - 1, which],
            device_id={"dp": peer},
            device_id_type=MESH,
        )

    def point_grad(which):
        up = grads[which].reshape(ticks * rows, chans)
        total = lax.dot_general(up, gels[which].reshape(ticks * rows, chans), TN, preferred_element_type=F32)
        pg_ref[which] = total
        pg_out[which] = total.astype(BF16)

    point_grad(1)
    for step_of in tap_rows(1):
        step_of()
    for hop in range(1, parties):
        swap(hop, 1).start()
    point_grad(0)
    for step_of in tap_rows(0):
        step_of()
    for hop in range(1, parties):
        swap(hop, 0).start()
    for which in range(2):
        for block in range(blocks):
            for row in range(SIDE):
                line = jnp.sum(sums[which, block, row], axis=1)
                at = slice(row * SIDE, (row + 1) * SIDE)
                dk_ref[which, at, lanes(block)] = line
    dk_out[...] = dk_ref[...].astype(BF16)
    for hop in range(1, parties):
        swap(hop, 2).start()
    for which in (1, 0, 2):
        for hop in range(1, parties):
            swap(hop, which).wait_recv()
    pg_in_ref[...] = pg_land[...]
    dk_in_ref[...] = dk_land[...]
    for which in (1, 0, 2):
        for hop in range(1, parties):
            swap(hop, which).wait_send()

    @pl.when(spot < sections - 1)
    def _():
        for tick in range(ticks - 1):
            for part in range(len(groups)):
                relay(tick, part).wait_send()


def finish_kernel(parties, final_in, pg_ref, pg_in_ref, dk_ref, dk_in_ref, final_ref, point_ref, depth_ref):
    me = lax.axis_index("dp")
    share = point_ref.shape[1]
    final_ref[...] = final_in[...]
    for which in range(2):
        total = pg_ref[which, pl.ds(pl.multiple_of(me * share, 16), share)]
        for hop in range(parties - 1):
            total = total + pg_in_ref[hop, which].astype(F32)
        point_ref[which] = total
        depth = dk_ref[which]
        for hop in range(parties - 1):
            depth = depth + dk_in_ref[hop, which].astype(F32)
        for party in range(parties):

            @pl.when(me == party)
            def _():
                depth_ref[:, which] = depth[:, party * share : (party + 1) * share]


def body(pipe_maps, fresh_maps, teacher_weight, student_depth, student_point):
    _, _, height, width, chans = pipe_maps.shape
    rows = height * width
    blocks = chans // LANES
    pair = 2 * height
    units = rows // pair
    ticks = fresh_maps.shape[0] + 1
    sections, parties = lax.axis_size("section"), lax.axis_size("dp")
    share = chans // parties
    peers = max(parties - 1, 1)
    hbm = pl.BlockSpec(memory_space=pltpu.HBM)
    vmem = pl.BlockSpec(memory_space=pltpu.VMEM)
    dma = pltpu.SemaphoreType.DMA
    pad_shape = pltpu.VMEM((blocks, (2 * width + 1) * height, LANES), F32)
    src_shape = pltpu.VMEM((blocks, SIDE, units + 6, height, 2 * LANES), BF16)
    map_shape = pltpu.VMEM((rows, chans), F32)
    taps = SIDE * SIDE
    results = (
        jax.ShapeDtypeStruct((height, width, chans), BF16),
        jax.ShapeDtypeStruct((2, chans, chans), F32),
        jax.ShapeDtypeStruct((peers, 2, share, chans), BF16),
        jax.ShapeDtypeStruct((2, taps, chans), F32),
        jax.ShapeDtypeStruct((peers, 2, taps, chans), BF16),
    )
    outs = pl.pallas_call(
        functools.partial(step_kernel, height, units // 2, ticks, sections, parties),
        out_shape=results,
        in_specs=[hbm, hbm, hbm, vmem, hbm],
        out_specs=(vmem,) * len(results),
        scratch_shapes=[
            pltpu.VMEM((ticks, height, width, chans), BF16),
            pltpu.VMEM((2, 9 * chans, chans), BF16),
            pltpu.VMEM((2, chans, chans), BF16),
            dma((2,)),
            dma((2,)),
            dma,
            pltpu.VMEM((ticks, rows, chans), BF16),
            pltpu.VMEM((ticks - 1, rows, chans), BF16),
            dma((ticks - 1, 2)),
            dma((ticks - 1, 2)),
            pltpu.VMEM((2, chans, chans), BF16),
            pltpu.VMEM((peers, 2, share, chans), BF16),
            pltpu.VMEM((2, taps, chans), BF16),
            pltpu.VMEM((peers, 2, taps, chans), BF16),
            dma((peers, 3)),
            dma((peers, 3)),
            pltpu.VMEM((2, blocks, taps, height, 2 * LANES), BF16),
            pad_shape,
            pad_shape,
            src_shape,
            src_shape,
            src_shape,
            pltpu.VMEM((3, (units + 2) * pair, chans), BF16),
            map_shape,
            map_shape,
            pltpu.VMEM((blocks, units, height, 2 * LANES), BF16),
            map_shape,
            map_shape,
            map_shape,
            map_shape,
            pltpu.VMEM((2, ticks, rows, chans), BF16),
            pltpu.VMEM((2, ticks, rows, chans), BF16),
            pltpu.VMEM((2, blocks, SIDE, SIDE, height, LANES), F32),
        ],
        compiler_params=pltpu.CompilerParams(
            vmem_limit_bytes=44 << 20, collective_id=0, has_side_effects=True
        ),
        name="step",
    )(
        pipe_maps[0, 0],
        fresh_maps[:, 0],
        teacher_weight.reshape(2, 9 * chans, chans),
        student_depth.swapaxes(0, 1),
        student_point,
    )
    final, point_grad, depth_grad = pl.pallas_call(
        functools.partial(finish_kernel, parties),
        out_shape=(
            results[0],
            jax.ShapeDtypeStruct((2, share, chans), F32),
            jax.ShapeDtypeStruct((taps, 2, share), F32),
        ),
        in_specs=[vmem] * len(outs),
        out_specs=(vmem,) * 3,
        compiler_params=pltpu.CompilerParams(vmem_limit_bytes=6 << 20),
        name="finish",
    )(*outs)
    return final[None, None], point_grad.swapaxes(1, 2), depth_grad.swapaxes(0, 1)


def solution(mesh):
    placed = (
        P("section", "dp", None, None, None),
        P(None, "dp", None, None, None),
        P("section", None, None, None, None),
        P("section", None, None),
        P("section", None, None),
    )
    return jax.shard_map(
        body,
        mesh=mesh,
        in_specs=placed,
        out_specs=(
            P("section", "dp", None, None, None),
            P("section", None, "dp"),
            P("section", None, "dp"),
        ),
        check_vma=False,
    )
```

```python
import functools

import jax
import jax.numpy as jnp
from jax import lax
from jax.experimental import pallas as pl
from jax.experimental.pallas import tpu as pltpu
from jax.sharding import PartitionSpec as P

LANES = 128
F32 = jnp.float32
BF16 = jnp.bfloat16
MESH = pl.DeviceIdType.MESH
NT = (((1,), (1,)), ((), ()))
TN = (((0,), (0,)), ((), ()))
SIDE = 7


def lanes(block):
    return slice(block * LANES, (block + 1) * LANES)


def columns(block):
    return pl.ds(pl.multiple_of(block * LANES, LANES), LANES)


def put_padded(vals, pad_ref, height, first=0):
    units = vals.shape[0] // (2 * height)
    for block in range(vals.shape[1] // LANES):
        for unit in range(units):
            for half in range(2):
                at = (2 * unit + half) * height
                to = (2 * (unit + half * units) + 1) * height
                pad_ref[first + block, to : to + height] = vals[at : at + height, lanes(block)]


def get_padded(pad_ref, block, height, units):
    rows = []
    for unit in range(units):
        for half in range(2):
            at = (2 * (unit + half * units) + 1) * height
            rows.append(pad_ref[block, at : at + height])
    return jnp.concatenate(rows, axis=0)


def spread(pad_ref, put, height, units, reach, group=None):
    def one_row(row, carry):
        for block in group or range(pad_ref.shape[0]):

            def load(w):
                return pad_ref[block, pl.ds((2 * w + 1) * height + row - reach, height)]

            zero = jnp.zeros((height, LANES), F32)
            cols = [load(w) for w in range(2 * units)]
            low = [zero] * reach + cols[: units + reach]
            high = cols[units - reach :] + [zero] * reach
            for unit in range(units + 2 * reach):
                put(block, row, unit, low[unit], high[unit])
        return carry

    lax.fori_loop(0, 2 * reach + 1, one_row, 0)


def strips(out_ref):
    def put(block, row, unit, low, high):
        out_ref[block, row, unit] = jnp.concatenate([low, high], axis=1).astype(BF16)

    return put


def windows(out_ref, height):
    def put(block, row, unit, low, high):
        at = slice(unit * 2 * height, (unit + 1) * 2 * height)
        out_ref[row, at, lanes(block)] = jnp.concatenate([low, high], axis=0).astype(BF16)

    return put


def beside(vals, height):
    split = vals.reshape(-1, 2 * height, LANES)
    return jnp.concatenate([split[:, :height], split[:, height:]], axis=2)


def below(vals):
    return jnp.concatenate([vals[:, :, :LANES], vals[:, :, LANES:]], axis=1).reshape(-1, LANES)


def tap_sum(src_ref, block, coef_ref, which, start, count, flip):
    total = None
    for rows in ((0, 1, 2, 3), (4, 5, 6)):
        part = None
        for row in rows:
            strip = src_ref[block, row, pl.ds(start, count + 6)]
            acc = None
            for col in range(SIDE):
                tap = row * SIDE + col
                tap = 48 - tap if flip else tap
                term = strip[col : col + count] * coef_ref[which, block, tap][None]
                acc = term if acc is None else acc + term
            part = acc if part is None else part + acc
        wide = part.astype(F32)
        total = wide if total is None else total + wide
    return total


def gelu_pair(act):
    root = 0.7978845608028654
    cubic = root * 0.044715
    square = act * act
    tanh = jnp.tanh(act * (root + cubic * square))
    half = 0.5 + 0.5 * tanh
    slope = half + (half - half * half) * (act * (2.0 * root + 6.0 * cubic * square))
    return act * half, slope


def step_kernel(
    height, step, ticks, sections, parties,
    pipe_hbm, fresh_hbm, weight_hbm, taps_hbm, point_hbm,
    final_ref, pg_ref, pg_in_ref, dk_ref, dk_in_ref,
    raw, weight, taps_ref, point, raw_sem, weight_sem, taps_sem, point_sem,
    teach, land, send_sem, recv_sem,
    pg_out, pg_land, dk_out, dk_land, swap_send, swap_recv,
    coef, pad, hpad, src0, src1, src2, win, slope0, slope1, dact0, cur, acc, u_one, resid, gels, grads, sums,
):
    rows, chans = cur.shape
    blocks = chans // LANES
    pair = 2 * height
    units = rows // pair
    chunks = units // step
    share = chans // parties
    srcs, slopes = (src0, src1), (slope0, slope1)
    spot, me = lax.axis_index("section"), lax.axis_index("dp")
    barrier = pltpu.get_barrier_semaphore()

    @pl.when(spot > 0)
    def _():
        pl.semaphore_signal(barrier, inc=1, device_id={"section": spot - 1}, device_id_type=MESH)

    for hop in range(1, parties):
        peer = lax.rem(me + hop, parties)
        pl.semaphore_signal(barrier, inc=1, device_id={"dp": peer}, device_id_type=MESH)

    fetch_pipe = pltpu.make_async_copy(pipe_hbm, raw.at[0], raw_sem.at[0])
    fetch_fresh = pltpu.make_async_copy(fresh_hbm, raw.at[pl.ds(1, ticks - 1)], raw_sem.at[1])
    fetch_weight = [pltpu.make_async_copy(weight_hbm.at[i], weight.at[i], weight_sem.at[i]) for i in range(2)]
    fetch_taps = pltpu.make_async_copy(taps_hbm, taps_ref, taps_sem)
    fetch_point = pltpu.make_async_copy(point_hbm, point, point_sem)
    for fetch in (fetch_pipe, fetch_weight[0], fetch_weight[1], fetch_taps, fetch_point, fetch_fresh):
        fetch.start()

    def span(index):
        return pl.ds(pl.multiple_of(index * step * pair, step * pair), step * pair)

    zero = jnp.zeros((height, LANES), F32)
    for block in range(blocks):
        for at in range(0, pad.shape[1], pair):
            pad[block, at : at + height] = zero
            hpad[block, at : at + height] = zero
    sums[...] = jnp.zeros_like(sums)

    def take_raw(tick, group):
        for row in range(height):
            for block in group:
                line = raw[tick, row, :, lanes(block)].astype(F32)
                pad[block, pl.ds(height + row, 2 * units, stride=pair)] = line

    def keep_input(group):
        for block in group:
            cur[:, lanes(block)] = get_padded(pad, block, height, units)
        spread(pad, windows(win, height), height, units, 1, group)

    def half_rows(half):
        return slice(half * rows // 2, (half + 1) * rows // 2)

    def window(half, down, right, cols):
        start = right * pair + half * rows // 2
        return win[down, start : start + rows // 2, cols]

    def first_conv(block, half):
        spots = [(down, right) for down in range(3) for right in range(3)]
        left = jnp.concatenate([window(half, down, right, lanes(block)) for down, right in spots], axis=1)
        starts = [(3 * down + right) * chans + block * LANES for down, right in spots]
        deep = jnp.concatenate([weight[0, at : at + LANES] for at in starts], axis=0)
        part = jnp.dot(left, deep, preferred_element_type=F32)
        acc[half_rows(half)] = part if block == 0 else acc[half_rows(half)] + part

    def second_conv(cols, half, tick):
        spots = [(down, right) for down in range(3) for right in range(3)]
        left = jnp.concatenate([window(half, down, right, slice(None)) for down, right in spots], axis=1)
        part = jnp.dot(left, weight[1, :, cols], preferred_element_type=F32)
        teach[tick, half_rows(half), cols] = (0.8 * (cur[half_rows(half), cols] + part)).astype(BF16)

    def keep_hidden():
        put_padded(jnp.maximum(acc[...], 0.0), hpad, height)
        spread(hpad, windows(win, height), height, units, 1)

    early = list(range(max(1, 2 * blocks // 3)))
    groups = [early, [block for block in range(blocks) if block not in early]]
    groups = [group for group in groups if group]

    def group_columns(group):
        return slice(group[0] * LANES, (group[-1] + 1) * LANES)

    def relay(tick, part):
        cols = group_columns(groups[part])
        return pltpu.make_async_remote_copy(
            src_ref=teach.at[tick, :, cols],
            dst_ref=land.at[tick, :, cols],
            send_sem=send_sem.at[tick, part],
            recv_sem=recv_sem.at[tick, part],
            device_id={"section": lax.rem(spot + 1, sections)},
            device_id_type=MESH,
        )

    def send(tick, part):
        @pl.when(spot < sections - 1)
        def _():
            relay(tick, part).start()

    def mix(main, side):
        done = 0
        for at, step_of in enumerate(main):
            upto = len(side) * (at + 1) // len(main)
            for other in side[done:upto]:
                other()
            done = upto
            step_of()

    def run_first(part, side):
        main = [functools.partial(first_conv, block, half) for block in groups[part] for half in range(2)]
        mix(main, side)

    def run_second(part, tick, side):
        cols = group_columns(groups[part])
        mix([functools.partial(second_conv, cols, half, tick) for half in range(2)], side)

    def back_point(which, tick):
        dgel = lax.dot_general(grads[which, tick], point[which], NT, preferred_element_type=F32)
        return dgel * slopes[which][...]

    def forward(which, tick):
        def chunk(at, carry):
            block, index = at // chunks, lax.rem(at, chunks)
            act = tap_sum(srcs[which], block, coef, which, index * step, step, False)
            gel, slope = gelu_pair(below(act))
            slopes[which][span(index), columns(block)] = slope
            gels[which, tick, span(index), columns(block)] = gel.astype(BF16)
            return carry

        lax.fori_loop(0, blocks * chunks, chunk, 0)
        return jnp.dot(gels[which, tick], point[which], preferred_element_type=F32)

    def student(tick):
        spread(pad, strips(src0), height, units, 3)
        middle = forward(0, tick) + cur[...]
        u_one[...] = middle
        put_padded(middle, pad, height)
        spread(pad, strips(src1), height, units, 3)
        diff = forward(1, tick) + u_one[...] - teach[tick].astype(F32)
        left = diff * (4.0 / rows)
        resid[...] = left
        grads[1, tick] = left.astype(BF16)
        put_padded(back_point(1, tick), pad, height)
        spread(pad, strips(src2), height, units, 3)

        def chunk_back(at, carry):
            block, index = at // chunks, lax.rem(at, chunks)
            back = tap_sum(src2, block, coef, 1, index * step, step, True)
            back = below(back) + resid[span(index), columns(block)]
            grads[0, tick, span(index), columns(block)] = back.astype(BF16)
            return carry

        lax.fori_loop(0, blocks * chunks, chunk_back, 0)
        dact = back_point(0, tick)
        for block in range(blocks):
            dact0[block] = beside(dact[:, lanes(block)], height).astype(BF16)

    def tap_row(which, block, row):
        part = src2[block, 3, 3 : 3 + units] if which else dact0[block]
        strip = srcs[which][block, row]
        for col in range(SIDE):
            prod = strip[col : col + units] * part
            size = units
            while size > 1:
                size //= 2
                prod = prod[:size] + prod[size:]
            wide = prod[0].astype(F32)
            sums[which, block, row, col] += wide[:, :LANES] + wide[:, LANES:]

    def tap_rows(which):
        return [functools.partial(tap_row, which, block, row) for block in range(blocks) for row in range(SIDE)]

    def share_out(steps):
        cut = [0]
        for group in groups:
            cut.append(cut[-1] + len(group) * len(steps) // blocks)
        return [steps[cut[i] : cut[i + 1]] for i in range(len(groups))]

    fetch_pipe.wait()
    take_raw(0, range(blocks))
    keep_input(range(blocks))
    fetch_weight[0].wait()
    for part in range(len(groups)):
        run_first(part, [])
    keep_hidden()
    fetch_weight[1].wait()
    pl.semaphore_wait(barrier, parties - 1 + (spot < sections - 1).astype(jnp.int32))
    for part in range(len(groups)):
        run_second(part, 0, [])
        send(0, part)
    fetch_taps.wait()
    for which in range(2):
        for block in range(blocks):
            for tap in range(SIDE * SIDE):
                line = jnp.broadcast_to(taps_ref[tap, which : which + 1, lanes(block)], (height, LANES))
                coef[which, block, tap] = jnp.concatenate([line, line], axis=1).astype(BF16)
    fetch_point.wait()
    fetch_fresh.wait()

    def tick_body(tick, carry):
        student(tick)
        sides = share_out(tap_rows(1))
        for part, group in enumerate(groups):

            @pl.when(spot > 0)
            def _():
                relay(tick, part).wait_recv()
                put_padded(land[tick, :, group_columns(group)].astype(F32), pad, height, group[0])

            @pl.when(spot == 0)
            def _():
                take_raw(tick + 1, group)

            keep_input(group)
            run_first(part, sides[part])
        keep_hidden()
        steps = tap_rows(0)
        for part in range(len(groups)):
            many = len(steps) // len(groups)
            run_second(part, tick + 1, steps[part * many : (part + 1) * many if part + 1 < len(groups) else len(steps)])

            @pl.when(tick + 1 < ticks - 1)
            def _():
                send(tick + 1, part)

        return carry

    lax.fori_loop(0, ticks - 1, tick_body, 0)
    last = ticks - 1
    for block in range(blocks):
        hpad_rows = teach[last, :, lanes(block)].astype(F32)
        for unit in range(units):
            for half in range(2):
                at = (2 * unit + half) * height
                to = (2 * (unit + half * units) + 1) * height
                hpad[block, to : to + height] = hpad_rows[at : at + height]
    for row in range(height):
        parts = [hpad[block, pl.ds(height + row, 2 * units, stride=pair)] for block in range(blocks)]
        final_ref[row] = jnp.concatenate(parts, axis=1).astype(BF16)
    student(last)

    def swap(hop, which):
        src, dst = (dk_out, dk_land.at[hop - 1]) if which == 2 else (None, None)
        peer = lax.rem(me + hop, parties)
        if src is None:
            src = pg_out.at[which, pl.ds(pl.multiple_of(peer * share, 16), share)]
            dst = pg_land.at[hop - 1, which]
        return pltpu.make_async_remote_copy(
            src_ref=src,
            dst_ref=dst,
            send_sem=swap_send.at[hop - 1, which],
            recv_sem=swap_recv.at[hop - 1, which],
            device_id={"dp": peer},
            device_id_type=MESH,
        )

    def point_grad(which):
        up = grads[which].reshape(ticks * rows, chans)
        total = lax.dot_general(up, gels[which].reshape(ticks * rows, chans), TN, preferred_element_type=F32)
        pg_ref[which] = total
        pg_out[which] = total.astype(BF16)

    point_grad(1)
    for step_of in tap_rows(1):
        step_of()
    for hop in range(1, parties):
        swap(hop, 1).start()
    point_grad(0)
    for step_of in tap_rows(0):
        step_of()
    for hop in range(1, parties):
        swap(hop, 0).start()
    for which in range(2):
        for block in range(blocks):
            for row in range(SIDE):
                line = jnp.sum(sums[which, block, row], axis=1)
                at = slice(row * SIDE, (row + 1) * SIDE)
                dk_ref[which, at, lanes(block)] = line
    dk_out[...] = dk_ref[...].astype(BF16)
    for hop in range(1, parties):
        swap(hop, 2).start()
    for which in (1, 0, 2):
        for hop in range(1, parties):
            swap(hop, which).wait_recv()
    pg_in_ref[...] = pg_land[...]
    dk_in_ref[...] = dk_land[...]
    for which in (1, 0, 2):
        for hop in range(1, parties):
            swap(hop, which).wait_send()

    @pl.when(spot < sections - 1)
    def _():
        for tick in range(ticks - 1):
            for part in range(len(groups)):
                relay(tick, part).wait_send()


def finish_kernel(parties, final_in, pg_ref, pg_in_ref, dk_ref, dk_in_ref, final_ref, point_ref, depth_ref):
    me = lax.axis_index("dp")
    share = point_ref.shape[1]
    final_ref[...] = final_in[...]
    for which in range(2):
        total = pg_ref[which, pl.ds(pl.multiple_of(me * share, 16), share)]
        for hop in range(parties - 1):
            total = total + pg_in_ref[hop, which].astype(F32)
        point_ref[which] = total
        depth = dk_ref[which]
        for hop in range(parties - 1):
            depth = depth + dk_in_ref[hop, which].astype(F32)
        for party in range(parties):

            @pl.when(me == party)
            def _():
                depth_ref[:, which] = depth[:, party * share : (party + 1) * share]


def body(pipe_maps, fresh_maps, teacher_weight, student_depth, student_point):
    _, _, height, width, chans = pipe_maps.shape
    rows = height * width
    blocks = chans // LANES
    pair = 2 * height
    units = rows // pair
    ticks = fresh_maps.shape[0] + 1
    sections, parties = lax.axis_size("section"), lax.axis_size("dp")
    share = chans // parties
    peers = max(parties - 1, 1)
    hbm = pl.BlockSpec(memory_space=pltpu.HBM)
    vmem = pl.BlockSpec(memory_space=pltpu.VMEM)
    dma = pltpu.SemaphoreType.DMA
    pad_shape = pltpu.VMEM((blocks, (2 * width + 1) * height, LANES), F32)
    src_shape = pltpu.VMEM((blocks, SIDE, units + 6, height, 2 * LANES), BF16)
    map_shape = pltpu.VMEM((rows, chans), F32)
    taps = SIDE * SIDE
    results = (
        jax.ShapeDtypeStruct((height, width, chans), BF16),
        jax.ShapeDtypeStruct((2, chans, chans), F32),
        jax.ShapeDtypeStruct((peers, 2, share, chans), BF16),
        jax.ShapeDtypeStruct((2, taps, chans), F32),
        jax.ShapeDtypeStruct((peers, 2, taps, chans), BF16),
    )
    outs = pl.pallas_call(
        functools.partial(step_kernel, height, units // 2, ticks, sections, parties),
        out_shape=results,
        in_specs=[hbm] * 5,
        out_specs=(vmem,) * len(results),
        scratch_shapes=[
            pltpu.VMEM((ticks, height, width, chans), BF16),
            pltpu.VMEM((2, 9 * chans, chans), BF16),
            pltpu.VMEM((taps, 2, chans), F32),
            pltpu.VMEM((2, chans, chans), BF16),
            dma((2,)),
            dma((2,)),
            dma,
            dma,
            pltpu.VMEM((ticks, rows, chans), BF16),
            pltpu.VMEM((ticks - 1, rows, chans), BF16),
            dma((ticks - 1, 2)),
            dma((ticks - 1, 2)),
            pltpu.VMEM((2, chans, chans), BF16),
            pltpu.VMEM((peers, 2, share, chans), BF16),
            pltpu.VMEM((2, taps, chans), BF16),
            pltpu.VMEM((peers, 2, taps, chans), BF16),
            dma((peers, 3)),
            dma((peers, 3)),
            pltpu.VMEM((2, blocks, taps, height, 2 * LANES), BF16),
            pad_shape,
            pad_shape,
            src_shape,
            src_shape,
            src_shape,
            pltpu.VMEM((3, (units + 2) * pair, chans), BF16),
            map_shape,
            map_shape,
            pltpu.VMEM((blocks, units, height, 2 * LANES), BF16),
            map_shape,
            map_shape,
            map_shape,
            map_shape,
            pltpu.VMEM((2, ticks, rows, chans), BF16),
            pltpu.VMEM((2, ticks, rows, chans), BF16),
            pltpu.VMEM((2, blocks, SIDE, SIDE, height, LANES), F32),
        ],
        compiler_params=pltpu.CompilerParams(
            vmem_limit_bytes=44 << 20, collective_id=0, has_side_effects=True
        ),
        name="step",
    )(
        pltpu.with_memory_space_constraint(pipe_maps[0, 0], pltpu.HBM),
        pltpu.with_memory_space_constraint(fresh_maps[:, 0], pltpu.HBM),
        pltpu.with_memory_space_constraint(teacher_weight.reshape(2, 9 * chans, chans), pltpu.HBM),
        pltpu.with_memory_space_constraint(student_depth.swapaxes(0, 1), pltpu.HBM),
        pltpu.with_memory_space_constraint(student_point, pltpu.HBM),
    )
    final, point_grad, depth_grad = pl.pallas_call(
        functools.partial(finish_kernel, parties),
        out_shape=(
            results[0],
            jax.ShapeDtypeStruct((2, share, chans), F32),
            jax.ShapeDtypeStruct((taps, 2, share), F32),
        ),
        in_specs=[vmem] * len(outs),
        out_specs=(vmem,) * 3,
        compiler_params=pltpu.CompilerParams(vmem_limit_bytes=6 << 20),
        name="finish",
    )(*outs)
    return final[None, None], point_grad.swapaxes(1, 2), depth_grad.swapaxes(0, 1)


def solution(mesh):
    placed = (
        P("section", "dp", None, None, None),
        P(None, "dp", None, None, None),
        P("section", None, None, None, None),
        P("section", None, None),
        P("section", None, None),
    )
    return jax.shard_map(
        body,
        mesh=mesh,
        in_specs=placed,
        out_specs=(
            P("section", "dp", None, None, None),
            P("section", None, "dp"),
            P("section", None, "dp"),
        ),
        check_vma=False,
    )
```

```python
import functools

import jax
import jax.numpy as jnp
from jax import lax
from jax.experimental import pallas as pl
from jax.experimental.pallas import tpu as pltpu
from jax.sharding import PartitionSpec as P

LANES = 128
F32 = jnp.float32
BF16 = jnp.bfloat16
MESH = pl.DeviceIdType.MESH
NT = (((1,), (1,)), ((), ()))
TN = (((0,), (0,)), ((), ()))
SIDE = 7


def lanes(block):
    return slice(block * LANES, (block + 1) * LANES)


def columns(block):
    return pl.ds(pl.multiple_of(block * LANES, LANES), LANES)


def put_padded(vals, pad_ref, height, first=0):
    units = vals.shape[0] // (2 * height)
    for block in range(vals.shape[1] // LANES):
        for unit in range(units):
            for half in range(2):
                at = (2 * unit + half) * height
                to = (2 * (unit + half * units) + 1) * height
                pad_ref[first + block, to : to + height] = vals[at : at + height, lanes(block)]


def get_padded(pad_ref, block, height, units):
    rows = []
    for unit in range(units):
        for half in range(2):
            at = (2 * (unit + half * units) + 1) * height
            rows.append(pad_ref[block, at : at + height])
    return jnp.concatenate(rows, axis=0)


def spread(pad_ref, put, height, units, reach, group=None):
    def one_row(row, carry):
        for block in group or range(pad_ref.shape[0]):

            def load(w):
                return pad_ref[block, pl.ds((2 * w + 1) * height + row - reach, height)]

            zero = jnp.zeros((height, LANES), F32)
            cols = [load(w) for w in range(2 * units)]
            low = [zero] * reach + cols[: units + reach]
            high = cols[units - reach :] + [zero] * reach
            for unit in range(units + 2 * reach):
                put(block, row, unit, low[unit], high[unit])
        return carry

    lax.fori_loop(0, 2 * reach + 1, one_row, 0)


def strips(out_ref):
    def put(block, row, unit, low, high):
        out_ref[block, row, unit] = jnp.concatenate([low, high], axis=1).astype(BF16)

    return put


def windows(out_ref, height):
    def put(block, row, unit, low, high):
        at = slice(unit * 2 * height, (unit + 1) * 2 * height)
        out_ref[row, at, lanes(block)] = jnp.concatenate([low, high], axis=0).astype(BF16)

    return put


def beside(vals, height):
    split = vals.reshape(-1, 2 * height, LANES)
    return jnp.concatenate([split[:, :height], split[:, height:]], axis=2)


def below(vals):
    return jnp.concatenate([vals[:, :, :LANES], vals[:, :, LANES:]], axis=1).reshape(-1, LANES)


def tap_sum(src_ref, block, coef_ref, which, start, count, flip):
    total = None
    for rows in ((0, 1, 2, 3), (4, 5, 6)):
        part = None
        for row in rows:
            strip = src_ref[block, row, pl.ds(start, count + 6)]
            acc = None
            for col in range(SIDE):
                tap = row * SIDE + col
                tap = 48 - tap if flip else tap
                term = strip[col : col + count] * coef_ref[which, block, tap][None]
                acc = term if acc is None else acc + term
            part = acc if part is None else part + acc
        wide = part.astype(F32)
        total = wide if total is None else total + wide
    return total


def gelu_pair(act):
    root = 0.7978845608028654
    cubic = root * 0.044715
    square = act * act
    tanh = jnp.tanh(act * (root + cubic * square))
    half = 0.5 + 0.5 * tanh
    slope = half + (half - half * half) * (act * (2.0 * root + 6.0 * cubic * square))
    return act * half, slope


def step_kernel(
    height, step, ticks, sections, parties,
    pipe_hbm, fresh_hbm, weight_hbm, taps_hbm, point_hbm,
    final_ref, pg_ref, pg_in_ref, dk_ref, dk_in_ref,
    raw, weight, taps_ref, point, raw_sem, weight_sem, taps_sem, point_sem,
    teach, land, send_sem, recv_sem,
    pg_out, pg_land, dk_out, dk_land, swap_send, swap_recv,
    coef, pad, hpad, src0, src1, src2, win, slope0, slope1, dact0, cur, acc, u_one, resid, gels, grads, sums,
):
    rows, chans = cur.shape
    blocks = chans // LANES
    pair = 2 * height
    units = rows // pair
    chunks = units // step
    share = chans // parties
    srcs, slopes = (src0, src1), (slope0, slope1)
    spot, me = lax.axis_index("section"), lax.axis_index("dp")
    barrier = pltpu.get_barrier_semaphore()

    @pl.when(spot > 0)
    def _():
        pl.semaphore_signal(barrier, inc=1, device_id={"section": spot - 1}, device_id_type=MESH)

    for hop in range(1, parties):
        peer = lax.rem(me + hop, parties)
        pl.semaphore_signal(barrier, inc=1, device_id={"dp": peer}, device_id_type=MESH)

    fetch_pipe = pltpu.make_async_copy(pipe_hbm, raw.at[0], raw_sem.at[0])
    fetch_fresh = pltpu.make_async_copy(fresh_hbm, raw.at[pl.ds(1, ticks - 1)], raw_sem.at[1])
    fetch_weight = [pltpu.make_async_copy(weight_hbm.at[i], weight.at[i], weight_sem.at[i]) for i in range(2)]
    fetch_taps = pltpu.make_async_copy(taps_hbm, taps_ref, taps_sem)
    fetch_point = pltpu.make_async_copy(point_hbm, point, point_sem)
    for fetch in (fetch_pipe, fetch_weight[0], fetch_weight[1], fetch_taps, fetch_point, fetch_fresh):
        fetch.start()

    def span(index):
        return pl.ds(pl.multiple_of(index * step * pair, step * pair), step * pair)

    zero = jnp.zeros((height, LANES), F32)
    for block in range(blocks):
        for at in range(0, pad.shape[1], pair):
            pad[block, at : at + height] = zero
            hpad[block, at : at + height] = zero
    sums[...] = jnp.zeros_like(sums)
    pg_ref[...] = jnp.zeros_like(pg_ref)

    def take_raw(tick, group):
        for row in range(height):
            for block in group:
                line = raw[tick, row, :, lanes(block)].astype(F32)
                pad[block, pl.ds(height + row, 2 * units, stride=pair)] = line

    def keep_input(group):
        for block in group:
            cur[:, lanes(block)] = get_padded(pad, block, height, units)
        spread(pad, windows(win, height), height, units, 1, group)

    def half_rows(half):
        return slice(half * rows // 2, (half + 1) * rows // 2)

    def window(half, down, right, cols):
        start = right * pair + half * rows // 2
        return win[down, start : start + rows // 2, cols]

    def first_conv(block, half):
        spots = [(down, right) for down in range(3) for right in range(3)]
        left = jnp.concatenate([window(half, down, right, lanes(block)) for down, right in spots], axis=1)
        starts = [(3 * down + right) * chans + block * LANES for down, right in spots]
        deep = jnp.concatenate([weight[0, at : at + LANES] for at in starts], axis=0)
        part = jnp.dot(left, deep, preferred_element_type=F32)
        acc[half_rows(half)] = part if block == 0 else acc[half_rows(half)] + part

    def second_conv(cols, half, tick):
        spots = [(down, right) for down in range(3) for right in range(3)]
        left = jnp.concatenate([window(half, down, right, slice(None)) for down, right in spots], axis=1)
        part = jnp.dot(left, weight[1, :, cols], preferred_element_type=F32)
        teach[tick, half_rows(half), cols] = (0.8 * (cur[half_rows(half), cols] + part)).astype(BF16)

    def keep_hidden():
        put_padded(jnp.maximum(acc[...], 0.0), hpad, height)
        spread(hpad, windows(win, height), height, units, 1)

    early = list(range(max(1, 2 * blocks // 3)))
    groups = [early, [block for block in range(blocks) if block not in early]]
    groups = [group for group in groups if group]

    def group_columns(group):
        return slice(group[0] * LANES, (group[-1] + 1) * LANES)

    def relay(tick, part):
        cols = group_columns(groups[part])
        return pltpu.make_async_remote_copy(
            src_ref=teach.at[tick, :, cols],
            dst_ref=land.at[tick, :, cols],
            send_sem=send_sem.at[tick, part],
            recv_sem=recv_sem.at[tick, part],
            device_id={"section": lax.rem(spot + 1, sections)},
            device_id_type=MESH,
        )

    def mix(main, side):
        done = 0
        for at, step_of in enumerate(main):
            upto = len(side) * (at + 1) // len(main)
            for other in side[done:upto]:
                other()
            done = upto
            step_of()

    def run_first(part, side):
        main = [functools.partial(first_conv, block, half) for block in groups[part] for half in range(2)]
        mix(main, side)

    def split(steps, weights):
        cut = [len(steps) * sum(weights[:at]) // sum(weights) for at in range(len(weights) + 1)]
        return [steps[cut[at] : cut[at + 1]] for at in range(len(weights))]

    def run_second(tick, side, sends):
        sides = split(side, [1] * len(groups))
        for part, group in enumerate(groups):
            cols = group_columns(group)
            mix([functools.partial(second_conv, cols, half, tick) for half in range(2)], sides[part])

            @pl.when(sends)
            def _():
                relay(tick, part).start()

    def back_point(which, tick):
        dgel = lax.dot_general(grads[which, tick], point[which], NT, preferred_element_type=F32)
        return dgel * slopes[which][...]

    def forward(which, tick):
        def chunk(at, carry):
            block, index = at // chunks, lax.rem(at, chunks)
            act = tap_sum(srcs[which], block, coef, which, index * step, step, False)
            gel, slope = gelu_pair(below(act))
            slopes[which][span(index), columns(block)] = slope
            gels[which, tick, span(index), columns(block)] = gel.astype(BF16)
            return carry

        lax.fori_loop(0, blocks * chunks, chunk, 0, unroll=blocks)
        return jnp.dot(gels[which, tick], point[which], preferred_element_type=F32)

    def point_grad(which, tick):
        pg_ref[which] += lax.dot_general(grads[which, tick], gels[which, tick], TN, preferred_element_type=F32)

    def student(tick):
        spread(pad, strips(src0), height, units, 3)
        middle = forward(0, tick) + cur[...]
        u_one[...] = middle
        put_padded(middle, pad, height)
        spread(pad, strips(src1), height, units, 3)
        diff = forward(1, tick) + u_one[...] - teach[tick].astype(F32)
        left = diff * (4.0 / rows)
        resid[...] = left
        grads[1, tick] = left.astype(BF16)
        put_padded(back_point(1, tick), pad, height)
        spread(pad, strips(src2), height, units, 3)

        def chunk_back(at, carry):
            block, index = at // chunks, lax.rem(at, chunks)
            back = tap_sum(src2, block, coef, 1, index * step, step, True)
            back = below(back) + resid[span(index), columns(block)]
            grads[0, tick, span(index), columns(block)] = back.astype(BF16)
            return carry

        lax.fori_loop(0, blocks * chunks, chunk_back, 0, unroll=blocks)
        dact = back_point(0, tick)
        for block in range(blocks):
            dact0[block] = beside(dact[:, lanes(block)], height).astype(BF16)
        point_grad(1, tick)
        point_grad(0, tick)

    def tap_row(which, block, row):
        part = src2[block, 3, 3 : 3 + units] if which else dact0[block]
        strip = srcs[which][block, row]
        for col in range(SIDE):
            prod = strip[col : col + units] * part
            size = units
            while size > 1:
                size //= 2
                prod = prod[:size] + prod[size:]
            wide = prod[0].astype(F32)
            sums[which, block, row, col] += wide[:, :LANES] + wide[:, LANES:]

    def tap_rows(which):
        return [functools.partial(tap_row, which, block, row) for block in range(blocks) for row in range(SIDE)]

    fetch_pipe.wait()
    take_raw(0, range(blocks))
    keep_input(range(blocks))
    fetch_weight[0].wait()
    for part in range(len(groups)):
        run_first(part, [])
    keep_hidden()
    fetch_weight[1].wait()
    pl.semaphore_wait(barrier, parties - 1 + (spot < sections - 1).astype(jnp.int32))
    run_second(0, [], spot < sections - 1)
    fetch_taps.wait()
    for which in range(2):
        for block in range(blocks):
            for tap in range(SIDE * SIDE):
                line = jnp.broadcast_to(taps_ref[tap, which : which + 1, lanes(block)], (height, LANES))
                coef[which, block, tap] = jnp.concatenate([line, line], axis=1).astype(BF16)
    fetch_point.wait()
    fetch_fresh.wait()

    def tick_body(tick, carry):
        student(tick)
        sides = split(tap_rows(1), [len(group) for group in groups])
        for part, group in enumerate(groups):

            @pl.when(spot > 0)
            def _():
                relay(tick, part).wait_recv()
                put_padded(land[tick, :, group_columns(group)].astype(F32), pad, height, group[0])

            @pl.when(spot == 0)
            def _():
                take_raw(tick + 1, group)

            keep_input(group)
            run_first(part, sides[part])
        keep_hidden()
        run_second(tick + 1, tap_rows(0), (spot < sections - 1) & (tick + 1 < ticks - 1))
        return carry

    lax.fori_loop(0, ticks - 1, tick_body, 0)
    last = ticks - 1
    for block in range(blocks):
        hpad_rows = teach[last, :, lanes(block)].astype(F32)
        for unit in range(units):
            for half in range(2):
                at = (2 * unit + half) * height
                to = (2 * (unit + half * units) + 1) * height
                hpad[block, to : to + height] = hpad_rows[at : at + height]
    for row in range(height):
        parts = [hpad[block, pl.ds(height + row, 2 * units, stride=pair)] for block in range(blocks)]
        final_ref[row] = jnp.concatenate(parts, axis=1).astype(BF16)
    student(last)

    def swap(hop, which):
        src, dst = (dk_out, dk_land.at[hop - 1]) if which == 2 else (None, None)
        peer = lax.rem(me + hop, parties)
        if src is None:
            src = pg_out.at[which, pl.ds(pl.multiple_of(peer * share, 16), share)]
            dst = pg_land.at[hop - 1, which]
        return pltpu.make_async_remote_copy(
            src_ref=src,
            dst_ref=dst,
            send_sem=swap_send.at[hop - 1, which],
            recv_sem=swap_recv.at[hop - 1, which],
            device_id={"dp": peer},
            device_id_type=MESH,
        )

    pg_out[...] = pg_ref[...].astype(BF16)
    for which in (1, 0):
        for hop in range(1, parties):
            swap(hop, which).start()
    for which in (1, 0):
        for step_of in tap_rows(which):
            step_of()
    for which in range(2):
        for block in range(blocks):
            for row in range(SIDE):
                line = jnp.sum(sums[which, block, row], axis=1)
                at = slice(row * SIDE, (row + 1) * SIDE)
                dk_ref[which, at, lanes(block)] = line
    dk_out[...] = dk_ref[...].astype(BF16)
    for hop in range(1, parties):
        swap(hop, 2).start()
    for which in (1, 0, 2):
        for hop in range(1, parties):
            swap(hop, which).wait_recv()
    pg_in_ref[...] = pg_land[...]
    dk_in_ref[...] = dk_land[...]
    for which in (1, 0, 2):
        for hop in range(1, parties):
            swap(hop, which).wait_send()

    @pl.when(spot < sections - 1)
    def _():
        for tick in range(ticks - 1):
            for part in range(len(groups)):
                relay(tick, part).wait_send()


def finish_kernel(parties, final_in, pg_ref, pg_in_ref, dk_ref, dk_in_ref, final_ref, point_ref, depth_ref):
    me = lax.axis_index("dp")
    share = point_ref.shape[1]
    final_ref[...] = final_in[...]
    for which in range(2):
        total = pg_ref[which, pl.ds(pl.multiple_of(me * share, 16), share)]
        for hop in range(parties - 1):
            total = total + pg_in_ref[hop, which].astype(F32)
        point_ref[which] = total
        depth = dk_ref[which]
        for hop in range(parties - 1):
            depth = depth + dk_in_ref[hop, which].astype(F32)
        for party in range(parties):

            @pl.when(me == party)
            def _():
                depth_ref[:, which] = depth[:, party * share : (party + 1) * share]


def body(pipe_maps, fresh_maps, teacher_weight, student_depth, student_point):
    _, _, height, width, chans = pipe_maps.shape
    rows = height * width
    blocks = chans // LANES
    pair = 2 * height
    units = rows // pair
    ticks = fresh_maps.shape[0] + 1
    sections, parties = lax.axis_size("section"), lax.axis_size("dp")
    share = chans // parties
    peers = max(parties - 1, 1)
    hbm = pl.BlockSpec(memory_space=pltpu.HBM)
    vmem = pl.BlockSpec(memory_space=pltpu.VMEM)
    dma = pltpu.SemaphoreType.DMA
    pad_shape = pltpu.VMEM((blocks, (2 * width + 1) * height, LANES), F32)
    src_shape = pltpu.VMEM((blocks, SIDE, units + 6, height, 2 * LANES), BF16)
    map_shape = pltpu.VMEM((rows, chans), F32)
    taps = SIDE * SIDE
    results = (
        jax.ShapeDtypeStruct((height, width, chans), BF16),
        jax.ShapeDtypeStruct((2, chans, chans), F32),
        jax.ShapeDtypeStruct((peers, 2, share, chans), BF16),
        jax.ShapeDtypeStruct((2, taps, chans), F32),
        jax.ShapeDtypeStruct((peers, 2, taps, chans), BF16),
    )
    outs = pl.pallas_call(
        functools.partial(step_kernel, height, units // 2, ticks, sections, parties),
        out_shape=results,
        in_specs=[hbm] * 5,
        out_specs=(vmem,) * len(results),
        scratch_shapes=[
            pltpu.VMEM((ticks, height, width, chans), BF16),
            pltpu.VMEM((2, 9 * chans, chans), BF16),
            pltpu.VMEM((taps, 2, chans), F32),
            pltpu.VMEM((2, chans, chans), BF16),
            dma((2,)),
            dma((2,)),
            dma,
            dma,
            pltpu.VMEM((ticks, rows, chans), BF16),
            pltpu.VMEM((ticks - 1, rows, chans), BF16),
            dma((ticks - 1, 2)),
            dma((ticks - 1, 2)),
            pltpu.VMEM((2, chans, chans), BF16),
            pltpu.VMEM((peers, 2, share, chans), BF16),
            pltpu.VMEM((2, taps, chans), BF16),
            pltpu.VMEM((peers, 2, taps, chans), BF16),
            dma((peers, 3)),
            dma((peers, 3)),
            pltpu.VMEM((2, blocks, taps, height, 2 * LANES), BF16),
            pad_shape,
            pad_shape,
            src_shape,
            src_shape,
            src_shape,
            pltpu.VMEM((3, (units + 2) * pair, chans), BF16),
            map_shape,
            map_shape,
            pltpu.VMEM((blocks, units, height, 2 * LANES), BF16),
            map_shape,
            map_shape,
            map_shape,
            map_shape,
            pltpu.VMEM((2, ticks, rows, chans), BF16),
            pltpu.VMEM((2, ticks, rows, chans), BF16),
            pltpu.VMEM((2, blocks, SIDE, SIDE, height, LANES), F32),
        ],
        compiler_params=pltpu.CompilerParams(
            vmem_limit_bytes=44 << 20, collective_id=0, has_side_effects=True
        ),
        name="step",
    )(
        pltpu.with_memory_space_constraint(pipe_maps[0, 0], pltpu.HBM),
        pltpu.with_memory_space_constraint(fresh_maps[:, 0], pltpu.HBM),
        pltpu.with_memory_space_constraint(teacher_weight.reshape(2, 9 * chans, chans), pltpu.HBM),
        pltpu.with_memory_space_constraint(student_depth.swapaxes(0, 1), pltpu.HBM),
        pltpu.with_memory_space_constraint(student_point, pltpu.HBM),
    )
    final, point_grad, depth_grad = pl.pallas_call(
        functools.partial(finish_kernel, parties),
        out_shape=(
            results[0],
            jax.ShapeDtypeStruct((2, share, chans), F32),
            jax.ShapeDtypeStruct((taps, 2, share), F32),
        ),
        in_specs=[vmem] * len(outs),
        out_specs=(vmem,) * 3,
        compiler_params=pltpu.CompilerParams(vmem_limit_bytes=6 << 20),
        name="finish",
    )(*outs)
    return final[None, None], point_grad.swapaxes(1, 2), depth_grad.swapaxes(0, 1)


def solution(mesh):
    placed = (
        P("section", "dp", None, None, None),
        P(None, "dp", None, None, None),
        P("section", None, None, None, None),
        P("section", None, None),
        P("section", None, None),
    )
    return jax.shard_map(
        body,
        mesh=mesh,
        in_specs=placed,
        out_specs=(
            P("section", "dp", None, None, None),
            P("section", None, "dp"),
            P("section", None, "dp"),
        ),
        check_vma=False,
    )
```
